32 devices in a mesh: tok: 8 (over z, x), head: 4 (over y, core).
Axes of the slice: x: 2, y: 2, z: 4, core: 2. Of those that a mesh axis runs over, the one named last changes fastest.
Arguments:
- streams: bfloat16 [3072, 4, 2048], P('tok', None, 'head'), may hold values from -6 to 6
- hc_static: float32 [4, 6], replicated, may hold values from -0.5 to 1.5
- hc_proj: bfloat16 [2048, 6], P('head'), may hold values from -0.125 to 0.125
- w_qkv: bfloat16 [3, 2048, 2048], P(None, None, 'head'), may hold values from -0.25 to 0.25
- w_out: bfloat16 [2048, 2048], P('head'), may hold values from -0.125 to 0.125
- prefix_kv: bfloat16 [1024, 2, 2048], P('tok', None, 'head'), may hold values from -160 to 160
- lengths: int32 [32], replicated, may hold values from 1 to 1536, 3072 in all
- req_group: int32 [32], replicated, may hold values from 0 to 3
- prefix_group: int32 [8], replicated, may hold values from 0 to 3, as said below
Outputs:
- new_streams: bfloat16 [3072, 4, 2048], P('tok', None, 'head')
- suffix_kv: bfloat16 [3072, 2, 2048], P('tok', None, 'head')
The draws below stay inside these ranges and needn't reach their ends.
Inputs may be any that keep to these rules, and one draw needn't show every extreme that they name: `prefix_group`: each group number appears exactly 2 times. The lengths sum to 3072; the longest request has exactly 1536 tokens.
All inputs are finite; a program needn't handle non-finite values.
Results may differ from the reference program's by a relative error of at most 0.012.
The reference program's roundings to bfloat16 on the way count: a program that leaves them out, or rounds other values in their place, can miss the bound.
Values may be sent and summed in bfloat16 or wider, within the bound.
A program may use at most 192 MiB of HBM per device.

```python
import math
import jax
import jax.numpy as jnp
import numpy as np
from jax import lax

D = 2048
HEADS = 16
HD = 128
STREAMS = 4
GROUPS = 4
PBLK = 128
TOKENS = 3072
REQUESTS = 32
MOST = 1536
GBLOCKS = 2
PREFIX = 256
ALLP = 1024


def draw_prefix_kv(key, part):
    shape = (ALLP, 2, D)
    cached = jax.random.truncated_normal(jax.random.fold_in(key, 1), -4.0, 4.0, shape, jnp.float32) * 2.0
    return cached.astype(jnp.bfloat16)


def draw_prefix_group(key, part):
    return (jax.random.permutation(key, GBLOCKS * GROUPS) // GBLOCKS).astype(jnp.int32)


def touch_ends(drawn, stream_key, smallest, largest):
    shape = drawn.shape
    spot = [jax.random.randint(jax.random.fold_in(stream_key, axis), (), 0, shape[axis]) for axis in range(len(shape))]
    drawn = drawn.at[tuple(spot)].set(smallest)
    longest = shape.index(max(shape))
    spot[longest] = (spot[longest] + 1) % shape[longest]
    return drawn.at[tuple(spot)].set(largest)


def shard_levels(key, dims, cuts, least, largest):
    def one(dim, parts):
        draws = jax.random.uniform(jax.random.fold_in(jax.random.fold_in(key, 6), dim), (parts,), jnp.float32, least / len(cuts), largest / len(cuts))
        return jnp.repeat(jnp.exp(draws), dims[dim] // parts).reshape((-1,) + (1,) * (len(dims) - dim - 1))

    loudness = one(*cuts[0])
    for cut in cuts[1:]:
        loudness = loudness * one(*cut)
    return loudness


def profile(number_of, total, bound, lean):
    portions = [(1 << 20) // math.isqrt(rank ** lean) + 1 for rank in range(2, number_of + 1)]
    surplus, counts = total - bound - (number_of - 1), [1] * (number_of - 1)
    while surplus > 0:
        movable = [i for i in range(number_of - 1) if counts[i] < bound]
        pool, remaining = sum([portions[i] for i in movable]), surplus
        for i in movable:
            more = min(bound - counts[i], max(1, remaining * portions[i] // pool), surplus)
            counts[i] = counts[i] + more
            surplus = surplus - more
    return np.array([bound] + counts)


def uneven_parts(own_key, amount, total, reach, slope):
    if amount == 2:
        one = jax.random.randint(own_key, (), max(1, total - reach), min(reach, total - 1) + 1)
        return jnp.stack([one, total - one])
    sizes = jnp.asarray(profile(amount, total, reach, slope), jnp.int32)
    couples = (amount - 1) // 2
    donor, receiver = sizes[1:1 + 2 * couples:2], sizes[2:2 + 2 * couples:2]
    room = jnp.minimum(donor - 1, reach - receiver)
    passed = jax.random.randint(jax.random.fold_in(own_key, 1), (couples,), 0, 1 << 20) % (room + 1)
    sizes = sizes.at[1:1 + 2 * couples:2].set(donor - passed).at[2:2 + 2 * couples:2].set(receiver + passed)
    return sizes[jax.random.permutation(jax.random.fold_in(own_key, 2), amount)]


def normal_values(key, shape, width, most, split=(), dtype=jnp.bfloat16):
    loudness = shard_levels(key, shape, split, -0.22, 0.18) if split else 1.0
    drawn = jax.random.normal(key, shape, jnp.float32) * width * loudness
    return jnp.minimum(jnp.maximum(drawn, -most), most).astype(dtype)


def setup_inputs(seed: int = 0) -> dict:
    splits = jax.random.split(jax.random.key(seed), 10)
    return {
        "streams": normal_values(splits[0], (TOKENS, STREAMS, D), 1.0, 6.0, ((0, 8), (2, 4))),
        "hc_static": jnp.clip(jax.random.uniform(splits[1], (STREAMS, STREAMS + 2), jnp.float32, -0.5, 1.5), -0.5, 1.5),
        "hc_proj": normal_values(splits[2], (D, STREAMS + 2), D ** -0.5, 0.125, ((0, 4),)),
        "w_qkv": normal_values(splits[3], (3, D, D), (D // 4) ** -0.5, 0.25, ((2, 4),)),
        "w_out": normal_values(splits[4], (D, D), D ** -0.5, 0.125, ((0, 4),)),
        "prefix_kv": draw_prefix_kv(jax.random.fold_in(splits[9], 71), 0),
        "lengths": uneven_parts(splits[6], REQUESTS, TOKENS, MOST, 2).astype(jnp.int32),
        "req_group": touch_ends(jax.random.randint(splits[7], (REQUESTS,), 0, GROUPS), jax.random.fold_in(splits[7], 1), 0, GROUPS - 1).astype(jnp.int32),
        "prefix_group": draw_prefix_group(jax.random.fold_in(splits[9], 71), 0),
    }


EPSILON = 1e-05
MASKED = -1e+30
ROPE_BASE = 10000.0

def rotate(values_in, position):
    half = HD // 2
    freq = ROPE_BASE ** (-(jnp.arange(half).astype(jnp.float32) * 2.0 / HD))
    angles = position.astype(jnp.float32)[:, None] * freq[None, :]
    cosine = jnp.cos(angles)[:, None, :]
    sine = jnp.sin(angles)[:, None, :]
    first = values_in[..., :half]
    second = values_in[..., half:]
    return jnp.concatenate([first * cosine - second * sine, second * cosine + first * sine], -1)

def reference(streams, hc_static, hc_proj, w_qkv, w_out, prefix_kv, lengths, req_group, prefix_group):
    stream_f = streams.astype(jnp.float32)
    average = lax.optimization_barrier(jnp.mean(stream_f, -1, keepdims=True))
    spread = lax.optimization_barrier(jnp.mean((stream_f - average) ** 2, -1, keepdims=True))
    normal_streams = (stream_f - average) * lax.rsqrt(spread + EPSILON)
    dynamic = jnp.tanh(jnp.einsum('tnd,dc->tnc', normal_streams, hc_proj.astype(jnp.float32), precision=lax.Precision.HIGHEST))
    coeffs = hc_static.astype(jnp.float32)[None] + dynamic
    width_mix = coeffs[..., 0]
    stream_mix = coeffs[..., 1:1 + STREAMS]
    depth_gain = coeffs[..., 1 + STREAMS]
    mixed = jnp.einsum('tn,tnd->td', width_mix, stream_f, precision=lax.Precision.HIGHEST).astype(jnp.bfloat16)
    mixed_f = mixed.astype(jnp.float32)
    center = lax.optimization_barrier(jnp.mean(mixed_f, -1, keepdims=True))
    variance = lax.optimization_barrier(jnp.mean((mixed_f - center) ** 2, -1, keepdims=True))
    normed = ((mixed_f - center) * lax.rsqrt(variance + EPSILON)).astype(jnp.bfloat16)
    weight_cat = jnp.transpose(w_qkv, (1, 0, 2)).reshape(D, 3 * D)
    triple = jnp.dot(normed, weight_cat, preferred_element_type=jnp.float32).reshape(TOKENS, 3, HEADS, HD)
    finish = jnp.cumsum(lengths).astype(jnp.int32)
    starts = (finish - lengths).astype(jnp.int32)
    token_index = jnp.arange(TOKENS).astype(jnp.int32)
    request = lax.optimization_barrier(jnp.sum((finish[None, :] <= token_index[:, None]).astype(jnp.int32), 1)).astype(jnp.int32)
    start_of = starts[request]
    group_of = req_group[request]
    position = PREFIX + token_index - start_of
    queries = rotate(triple[:, 0], position).astype(jnp.bfloat16)
    keys_new = rotate(triple[:, 1], position).astype(jnp.bfloat16)
    values_new = triple[:, 2].astype(jnp.bfloat16)
    suffix_kv = jnp.stack([keys_new.reshape(TOKENS, D), values_new.reshape(TOKENS, D)], 1)
    owners = prefix_group[(jnp.arange(ALLP) // PBLK).astype(jnp.int32)]
    allowed = jnp.concatenate([group_of[:, None] == owners[None, :], (request[:, None] == request[None, :]) & (token_index[None, :] <= token_index[:, None])], 1)
    key_all = jnp.concatenate([prefix_kv[:, 0].reshape(ALLP, HEADS, HD), keys_new], 0)
    value_all = jnp.concatenate([prefix_kv[:, 1].reshape(ALLP, HEADS, HD), values_new], 0)
    scaling = HD ** (-0.5)

    def one_head(operands):
        query_h, key_h, value_h = operands
        scores = jnp.dot(query_h, key_h.T, preferred_element_type=jnp.float32) * scaling
        scores = jnp.where(allowed, scores, MASKED)
        top_score = lax.optimization_barrier(jnp.max(scores, 1, keepdims=True))
        weights = jnp.where(allowed, jnp.exp(scores - top_score), 0.0)
        totals = lax.optimization_barrier(jnp.sum(weights, 1, keepdims=True))
        return jnp.dot(weights.astype(jnp.bfloat16), value_h, preferred_element_type=jnp.float32) / totals
    heads_out = lax.map(one_head, (jnp.transpose(queries, (1, 0, 2)), jnp.transpose(key_all, (1, 0, 2)), jnp.transpose(value_all, (1, 0, 2))))
    attended = jnp.transpose(heads_out, (1, 0, 2)).reshape(TOKENS, D).astype(jnp.bfloat16)
    branch = jnp.dot(attended, w_out, preferred_element_type=jnp.float32)
    updated = jnp.einsum('tji,tjd->tid', stream_mix, stream_f, precision=lax.Precision.HIGHEST) + depth_gain[..., None] * branch[:, None, :]
    return (updated.astype(jnp.bfloat16), suffix_kv)
```

```python
import functools

import jax
import jax.numpy as jnp
from jax import lax
from jax.experimental import pallas as pl
from jax.experimental.pallas import tpu as pltpu
from jax.sharding import PartitionSpec as P

HD = 128
STREAMS = 4
GROUPS = 4
COLS = STREAMS + 2
MOST = 1536
BR = 128

EPSILON = 1e-05
MASKED = -1e30
ROPE_BASE = 10000.0
LOG2E = 1.4426950408889634
MESH = pl.DeviceIdType.MESH
NT = (((1,), (1,)), ((), ()))


def remote(src, dst, send_sem, recv_sem, axis, target):
    return pltpu.make_async_remote_copy(
        src_ref=src,
        dst_ref=dst,
        send_sem=send_sem,
        recv_sem=recv_sem,
        device_id={axis: target},
        device_id_type=MESH,
    )


def kernel(
    T, H, R, W, D,
    streams, hct, hstat, cosr, sinr, rowinfo, keyreq, prefgrp, prefix_in, wqkv_hbm, wout_hbm,
    out, kv_out,
    wqkv, wout, stat, stat_in, ctr, coef, mix, nrm, qb, kvb, pb, mb, lb, acc, upd, part, pair_out, pair_in, y_out, y_in,
    w_sem, stat_ss, stat_rs, mix_ys, mix_yr, mix_cs, mix_cr, pz_up, pz_dn, pp_s, p_r, kz_s, kp_s, k_r,
    ro_cs, ro_cr, ro_ys, ro_yr,
):
    NB = R // BR
    NH = W // HD
    Y = H // 2
    i = lax.axis_index("tok")
    h = lax.axis_index("head")
    core = lax.rem(h, 2)
    yy = h // 2
    other = h + 1 - 2 * core
    odd = lax.rem(i, 2)
    mate = i + 1 - 2 * odd
    has_up = i + 2 < T
    has_dn = i >= 2
    scaling = HD ** (-0.5) * LOG2E

    own_copy = pltpu.make_async_copy(prefix_in, pb.at[i], w_sem.at[2])
    own_copy.start()
    w_copy = pltpu.make_async_copy(wqkv_hbm, wqkv, w_sem.at[0])
    w_copy.start()
    wo_copy = pltpu.make_async_copy(wout_hbm, wout, w_sem.at[1])
    wo_copy.start()
    barrier = pltpu.get_barrier_semaphore()
    for k in range(1, H):
        pl.semaphore_signal(barrier, inc=1, device_id={"head": lax.rem(h + k, H)}, device_id_type=MESH)
    pl.semaphore_signal(barrier, inc=1, device_id={"tok": mate}, device_id_type=MESH)

    @pl.when(has_up)
    def _():
        pl.semaphore_signal(barrier, inc=1, device_id={"tok": i + 2}, device_id_type=MESH)

    @pl.when(has_dn)
    def _():
        pl.semaphore_signal(barrier, inc=1, device_id={"tok": i - 2}, device_id_type=MESH)

    pl.semaphore_wait(barrier, H + has_up.astype(jnp.int32) + has_dn.astype(jnp.int32))

    def pre_up(b):
        return remote(pb.at[b], pb.at[b], pz_up.at[b], p_r.at[b], "tok", i + 2)

    def pre_dn(b):
        return remote(pb.at[b], pb.at[b], pz_dn.at[b], p_r.at[b], "tok", i - 2)

    def pre_mate(b):
        return remote(pb.at[b], pb.at[b], pp_s.at[b], p_r.at[b], "tok", mate)

    own_copy.wait()

    @pl.when(has_up)
    def _():
        pre_up(i).start()

    @pl.when(has_dn)
    def _():
        pre_dn(i).start()

    pre_mate(i).start()
    STEPS = T // 2 - 1

    def pre_step(s):
        below = i - 2 * s
        above = i + 2 * s

        @pl.when(below >= 0)
        def _():
            pre_up(below).wait_recv()
            pre_mate(below).start()

            @pl.when(has_up)
            def _():
                pre_up(below).start()

        @pl.when(above < T)
        def _():
            pre_dn(above).wait_recv()
            pre_mate(above).start()

            @pl.when(has_dn)
            def _():
                pre_dn(above).start()

    ones_rows = jnp.ones((16, W), jnp.bfloat16)
    row_id = lax.broadcasted_iota(jnp.int32, (8, R), 0)
    base = hct[...]
    for j in range(STREAMS):
        s = streams[j]
        sf = s.astype(jnp.float32)
        sq = sf * sf
        hi = sq.astype(jnp.bfloat16)
        lo = (sq - hi.astype(jnp.float32)).astype(jnp.bfloat16)
        pr = lax.dot_general(base, s, NT, preferred_element_type=jnp.float32)
        sums = lax.dot_general(ones_rows, s, NT, preferred_element_type=jnp.float32)
        sqs = lax.dot_general(ones_rows, hi, NT, preferred_element_type=jnp.float32) + lax.dot_general(
            ones_rows, lo, NT, preferred_element_type=jnp.float32
        )
        stat[8 * j : 8 * j + 8, :] = jnp.where(row_id == 7, sqs[0:8], sums[0:8])
        stat[8 * j : 8 * j + COLS, :] = pr
    cs = lax.dot_general(base, jnp.ones((R, W), jnp.bfloat16), NT, preferred_element_type=jnp.float32)
    stat[32:40, :] = jnp.zeros((8, R), jnp.float32)
    stat[32 : 32 + COLS, :] = cs

    def stat_copy(k):
        return remote(stat, stat_in.at[k - 1], stat_ss.at[k - 1], stat_rs.at[k - 1], "head", lax.rem(h + k, H))

    for k in range(1, H):
        stat_copy(k).start()

    for k in range(1, H):
        stat_copy(k).wait_recv()
    next_step = 1
    if next_step <= STEPS:
        pre_step(next_step)
        next_step += 1
    total = stat[...]
    for k in range(1, H):
        total = total + stat_in[k - 1]
    ctr[...] = jnp.zeros_like(ctr)
    col_sum = total[32:40]
    for j in range(STREAMS):
        blk = total[8 * j : 8 * j + 8]
        average = blk[6:7] / D
        spread = blk[7:8] / D - average * average
        inv = lax.rsqrt(spread + EPSILON)
        static = jnp.zeros((8, R), jnp.float32)
        for c in range(COLS):
            static = jnp.where(row_id == c, hstat[j, c], static)
        ctr[8 * j : 8 * j + 8, :] = jnp.tanh((blk - average * col_sum) * inv) + static
    coef[...] = jnp.transpose(ctr[...])

    def mix_y(r, k):
        to = lax.rem(yy + k, Y) * 2 + core
        return remote(mix.at[r, h], mix.at[r, h], mix_ys.at[r, k - 1], mix_yr.at[r, k - 1], "head", to)

    def mix_core(r, k):
        piece = lax.rem(yy + Y - k, Y) * 2 + core
        return remote(mix.at[r, piece], mix.at[r, piece], mix_cs.at[r, k], mix_cr.at[r, k], "head", other)

    for r in range(NB):
        rows = slice(r * BR, (r + 1) * BR)
        total_mix = None
        for j in range(STREAMS):
            term = coef[rows, 8 * j : 8 * j + 1] * streams[j, rows, :].astype(jnp.float32)
            total_mix = term if total_mix is None else total_mix + term
        mix[r, h] = total_mix.astype(jnp.bfloat16)
        for k in range(1, Y):
            mix_y(r, k).start()
        mix_core(r, 0).start()

    def own_share(r):
        rows = slice(r * BR, (r + 1) * BR)
        for q in range(STREAMS):
            share = None
            for j in range(STREAMS):
                term = coef[rows, 8 * j + 1 + q : 8 * j + 2 + q] * streams[j, rows, :].astype(jnp.float32)
                share = term if share is None else share + term
            upd[q, rows, :] = share

    own_share(0)
    if next_step <= STEPS:
        pre_step(next_step)
        next_step += 1

    def kv_up_own(r):
        return remote(kvb.at[0, r], kvb.at[2, r], kz_s.at[0, r], k_r.at[2, r], "tok", i + 2)

    def kv_up_relay(r):
        return remote(kvb.at[2, r], kvb.at[4, r], kz_s.at[1, r], k_r.at[4, r], "tok", i + 2)

    def kv_mate(src, dst, r):
        return remote(kvb.at[src, r], kvb.at[dst, r], kp_s.at[src, r], k_r.at[dst, r], "tok", mate)

    def kv_wait(slot, r):
        remote(kvb.at[slot, r], kvb.at[slot, r], kz_s.at[0, r], k_r.at[slot, r], "tok", mate).wait_recv()

    for r in range(NB):
        rows = slice(r * BR, (r + 1) * BR)
        for k in range(1, Y):
            mix_y(r, k).wait_recv()
            mix_core(r, k).start()
        for k in range(Y):
            mix_core(r, k).wait_recv()
        if r == 0:
            w_copy.wait()
        summed = None
        for p in range(H):
            piece = jnp.sum(mix[r, p].astype(jnp.float32), -1, keepdims=True)
            summed = piece if summed is None else summed + piece
        center = summed / D
        squares = None
        for p in range(H):
            dev = mix[r, p].astype(jnp.float32) - center
            piece = jnp.sum(dev * dev, -1, keepdims=True)
            squares = piece if squares is None else squares + piece
        inv = lax.rsqrt(squares / D + EPSILON)
        for p in range(H):
            nrm[:, p * W : (p + 1) * W] = ((mix[r, p].astype(jnp.float32) - center) * inv).astype(jnp.bfloat16)
        c = cosr[rows, :]
        sn = sinr[rows, :]
        kk = jnp.dot(nrm[...], wqkv[1], preferred_element_type=jnp.float32)
        vv = jnp.dot(nrm[...], wqkv[2], preferred_element_type=jnp.float32)
        for n in range(NH):
            part_k = kk[:, n * HD : (n + 1) * HD]
            kvb[0, r, n, :, 0:HD] = (part_k * c + pltpu.roll(part_k, HD // 2, 1) * sn).astype(jnp.bfloat16)
            kvb[0, r, n, :, HD : 2 * HD] = vv[:, n * HD : (n + 1) * HD].astype(jnp.bfloat16)

        @pl.when(has_up)
        def _():
            kv_up_own(r).start()

        @pl.when(odd == 0)
        def _():
            kv_mate(0, 1, r).start()

        qq = jnp.dot(nrm[...], wqkv[0], preferred_element_type=jnp.float32)
        for n in range(NH):
            part_q = qq[:, n * HD : (n + 1) * HD]
            qb[n, r] = (part_q * c + pltpu.roll(part_q, HD // 2, 1) * sn).astype(jnp.bfloat16)
        if next_step <= STEPS:
            pre_step(next_step)
            next_step += 1
    while next_step <= STEPS:
        pre_step(next_step)
        next_step += 1

    def relay(r):
        @pl.when(has_dn)
        def _():
            kv_wait(2, r)

            @pl.when(has_up)
            def _():
                kv_up_relay(r).start()

            @pl.when(odd == 0)
            def _():
                kv_mate(2, 3, r).start()

            @pl.when(odd == 1)
            def _():
                kv_mate(2, 1, r).start()

    def relay_far(r):
        @pl.when(jnp.logical_and(odd == 1, i >= 4))
        def _():
            kv_wait(4, r)
            kv_mate(4, 3, r).start()

    def step(n, r, scores, values, first):
        top = jnp.max(scores, 1, keepdims=True)
        if first:
            new_max = top
        else:
            old = mb[n, r][:, 0:1]
            new_max = jnp.maximum(old, top)
        weights = jnp.exp2(scores - new_max)
        count = jnp.sum(weights, 1, keepdims=True)
        numer = jnp.dot(weights.astype(jnp.bfloat16), values, preferred_element_type=jnp.float32)
        if not first:
            scale = jnp.exp2(old - new_max)
            count = count + lb[n, r][:, 0:1] * scale
            numer = numer + acc[n, r] * scale
        mb[n, r] = jnp.broadcast_to(new_max, (BR, HD))
        lb[n, r] = jnp.broadcast_to(count, (BR, HD))
        acc[n, r] = numer

    def absorb(slot, r):
        at = pl.ds(pl.multiple_of(r * BR, BR), BR)
        allowed = rowinfo[at, 0:1] == keyreq[slot : slot + 1, :]
        if slot == 0:
            causal = lax.broadcasted_iota(jnp.int32, (BR, R), 1) <= lax.broadcasted_iota(
                jnp.int32, (BR, R), 0
            ) + r * BR
            allowed = jnp.logical_and(allowed, causal)
        for n in range(NH):
            kv = kvb[slot, :, n].reshape(R, 2 * HD)
            scores = lax.dot_general(qb[n, r], kv[:, 0:HD], NT, preferred_element_type=jnp.float32) * scaling
            step(n, r, jnp.where(allowed, scores, MASKED), kv[:, HD : 2 * HD], slot == 0)

    def over_all(body):
        def one(r, carry):
            body(r)
            return carry

        lax.fori_loop(0, NB, one, 0)

    PG = 4

    def absorb_prefix(g, r):
        at = pl.ds(pl.multiple_of(r * BR, BR), BR)
        lane_block = lax.broadcasted_iota(jnp.int32, (1, PG * BR), 1) // BR
        owner = jnp.zeros((1, PG * BR), jnp.int32)
        for b in range(PG):
            owner = jnp.where(lane_block == b, prefgrp[g * PG + b], owner)
        allowed = rowinfo[at, 1:2] == owner
        for n in range(NH):
            kv = pb[g * PG : (g + 1) * PG, n].reshape(PG * BR, 2 * HD)
            scores = lax.dot_general(qb[n, r], kv[:, 0:HD], NT, preferred_element_type=jnp.float32) * scaling
            step(n, r, jnp.where(allowed, scores, MASKED), kv[:, HD : 2 * HD], False)

    over_all(functools.partial(absorb, 0))
    relay(0)
    for b in range(T):
        @pl.when(lax.rem(b + i, 2) == 1)
        def _():
            pre_mate(b).wait_recv()
    groups = T // PG
    for g in range(groups):
        over_all(functools.partial(absorb_prefix, g))
        if g + 1 < NB:
            relay(g + 1)
    for r in range(groups + 1, NB):
        relay(r)

    for r in range(1, NB):
        own_share(r)
    for r in range(NB):
        kv_out[r] = kvb[0, r]

    @pl.when(has_dn)
    def _():
        over_all(functools.partial(absorb, 2))

    relay_far(0)

    @pl.when(i >= 1)
    def _():
        for r in range(NB):
            kv_wait(1, r)
        over_all(functools.partial(absorb, 1))

    for r in range(1, NB):
        relay_far(r)

    @pl.when(i >= 4)
    def _():
        @pl.when(odd == 0)
        def _():
            for r in range(NB):
                kv_wait(4, r)

        over_all(functools.partial(absorb, 4))

    @pl.when(i >= 3)
    def _():
        for r in range(NB):
            kv_wait(3, r)

    wo_copy.wait()

    def out_core(r):
        return remote(pair_out.at[r], pair_in.at[r], ro_cs.at[r], ro_cr.at[r], "head", other)

    def out_y(r, k):
        to = lax.rem(yy + k, Y)
        return remote(y_out.at[r, k - 1], y_in.at[r, k - 1], ro_ys.at[r, k - 1], ro_yr.at[r, k - 1], "head", to * 2 + core)

    def pair_sum(r):
        out_core(r).wait_recv()
        for k in range(1, Y):
            q = lax.rem(yy + k, Y)
            y_out[r, k - 1] = (part[2 * q + core, r] + pair_in[r, q].astype(jnp.float32)).astype(jnp.bfloat16)
            out_y(r, k).start()

    for r in range(NB):
        @pl.when(i >= 3)
        def _():
            absorb(3, r)

        for n in range(NH):
            nrm[:, n * HD : (n + 1) * HD] = (acc[n, r] / lb[n, r]).astype(jnp.bfloat16)
        partial_rows = jnp.dot(nrm[:, 0:W], wout[...], preferred_element_type=jnp.float32)
        for p in range(H):
            part[p, r] = partial_rows[:, p * W : (p + 1) * W]
        for q in range(Y):
            pair_out[r, q] = part[2 * q + 1 - core, r].astype(jnp.bfloat16)
        out_core(r).start()
        if r > 0:
            pair_sum(r - 1)
    pair_sum(NB - 1)
    for r in range(NB):
        rows = slice(r * BR, (r + 1) * BR)
        branch = part[h, r] + pair_in[r, yy].astype(jnp.float32)
        for k in range(1, Y):
            out_y(r, k).wait_recv()
            branch = branch + y_in[r, k - 1].astype(jnp.float32)
        for q in range(STREAMS):
            out[q, rows, :] = (upd[q, rows, :] + coef[rows, 8 * q + 5 : 8 * q + 6] * branch).astype(jnp.bfloat16)

    for k in range(1, H):
        stat_copy(k).wait_send()
    for r in range(NB):
        for k in range(1, Y):
            mix_y(r, k).wait_send()
        for k in range(Y):
            mix_core(r, k).wait_send()

        @pl.when(has_up)
        def _():
            kv_up_own(r).wait_send()

            @pl.when(has_dn)
            def _():
                kv_up_relay(r).wait_send()

        @pl.when(odd == 0)
        def _():
            kv_mate(0, 1, r).wait_send()

        @pl.when(has_dn)
        def _():
            kv_mate(2, 1, r).wait_send()

        @pl.when(jnp.logical_and(odd == 1, i >= 4))
        def _():
            kv_mate(4, 3, r).wait_send()

        out_core(r).wait_send()
        for k in range(1, Y):
            out_y(r, k).wait_send()

    @pl.when(has_up)
    def _():
        pre_up(i).wait_send()

    @pl.when(has_dn)
    def _():
        pre_dn(i).wait_send()

    pre_mate(i).wait_send()
    for s in range(1, STEPS + 1):
        below = i - 2 * s
        above = i + 2 * s

        @pl.when(below >= 0)
        def _():
            pre_mate(below).wait_send()

            @pl.when(has_up)
            def _():
                pre_up(below).wait_send()

        @pl.when(above < T)
        def _():
            pre_mate(above).wait_send()

            @pl.when(has_dn)
            def _():
                pre_dn(above).wait_send()


def shards(streams, hc_static, hc_proj, w_qkv, w_out, prefix_kv, lengths, req_group, prefix_group):
    R = streams.shape[0]
    W = streams.shape[2]
    D = w_qkv.shape[1]
    T = lax.axis_size("tok")
    H = lax.axis_size("head")
    NH = W // HD
    NB = R // BR
    Y = H // 2
    assert R % BR == 0 and 4 * R >= MOST and T % 4 == 0 and prefix_kv.shape[0] == BR
    tok = lax.axis_index("tok")
    row_base = tok * R
    prefix_len = prefix_kv.shape[0] * T // GROUPS
    order = jnp.arange(lengths.shape[0], dtype=jnp.int32)
    finish = jnp.sum(jnp.where(order[None, :] <= order[:, None], lengths[None, :], 0), 1)
    starts = finish - lengths
    global_rows = row_base + jnp.arange(R, dtype=jnp.int32)

    def request_of(positions):
        return jnp.sum((finish[None, :] <= positions[:, None]).astype(jnp.int32), 1)

    request = request_of(global_rows)
    onehot = (request[:, None] == jnp.arange(lengths.shape[0], dtype=jnp.int32)[None, :]).astype(jnp.int32)
    start_of = jnp.sum(onehot * starts[None, :], 1)
    group_of = jnp.sum(onehot * req_group[None, :], 1)
    position = prefix_len + global_rows - start_of
    half = HD // 2
    freq = ROPE_BASE ** (-(jnp.arange(half).astype(jnp.float32) * 2.0 / HD))
    angles = position.astype(jnp.float32)[:, None] * freq[None, :]
    cosine = jnp.cos(angles)
    sine = jnp.sin(angles)
    cosr = jnp.concatenate([cosine, cosine], 1)
    sinr = jnp.concatenate([-sine, sine], 1)
    lane = jnp.arange(128, dtype=jnp.int32)[None, :]
    rowinfo = jnp.where(lane == 0, request[:, None], group_of[:, None])
    back = jnp.arange(8, dtype=jnp.int32)[:, None] * R
    key_pos = global_rows[None, :] - back
    keyreq = jnp.sum((finish[None, None, :] <= key_pos[:, :, None]).astype(jnp.int32), 2)
    streams_t = jnp.transpose(streams, (1, 0, 2))
    prefix_t = jnp.transpose(prefix_kv.reshape(BR, 2, NH, HD), (2, 0, 1, 3)).reshape(NH, BR, 2 * HD)

    vm = pl.BlockSpec(memory_space=pltpu.VMEM)
    sm = pl.BlockSpec(memory_space=pltpu.SMEM)
    hbm = pl.BlockSpec(memory_space=pl.ANY)
    dma = pltpu.SemaphoreType.DMA
    bf, f32 = jnp.bfloat16, jnp.float32
    new_t, kv = pl.pallas_call(
        functools.partial(kernel, T, H, R, W, D),
        out_shape=(
            jax.ShapeDtypeStruct((STREAMS, R, W), bf),
            jax.ShapeDtypeStruct((NB, NH, BR, 2 * HD), bf),
        ),
        in_specs=[vm, vm, sm, vm, vm, vm, vm, sm, vm, hbm, hbm],
        out_specs=(vm, vm),
        scratch_shapes=[
            pltpu.VMEM((3, D, W), bf),
            pltpu.VMEM((W, D), bf),
            pltpu.VMEM((40, R), f32),
            pltpu.VMEM((H - 1, 40, R), f32),
            pltpu.VMEM((128, R), f32),
            pltpu.VMEM((R, 128), f32),
            pltpu.VMEM((NB, H, BR, W), bf),
            pltpu.VMEM((BR, D), bf),
            pltpu.VMEM((NH, NB, BR, HD), bf),
            pltpu.VMEM((5, NB, NH, BR, 2 * HD), bf),
            pltpu.VMEM((T, NH, BR, 2 * HD), bf),
            pltpu.VMEM((NH, NB, BR, HD), f32),
            pltpu.VMEM((NH, NB, BR, HD), f32),
            pltpu.VMEM((NH, NB, BR, HD), f32),
            pltpu.VMEM((STREAMS, R, W), f32),
            pltpu.VMEM((H, NB, BR, W), f32),
            pltpu.VMEM((NB, Y, BR, W), bf),
            pltpu.VMEM((NB, Y, BR, W), bf),
            pltpu.VMEM((NB, Y - 1, BR, W), bf),
            pltpu.VMEM((NB, Y - 1, BR, W), bf),
            dma((3,)),
            dma((H - 1,)),
            dma((H - 1,)),
            dma((NB, Y - 1)),
            dma((NB, Y - 1)),
            dma((NB, Y)),
            dma((NB, Y)),
            dma((T,)),
            dma((T,)),
            dma((T,)),
            dma((T,)),
            dma((2, NB)),
            dma((5, NB)),
            dma((5, NB)),
            dma((NB,)),
            dma((NB,)),
            dma((NB, Y - 1)),
            dma((NB, Y - 1)),
        ],
        compiler_params=pltpu.CompilerParams(
            collective_id=0, has_side_effects=True, vmem_limit_bytes=56 * 1024 * 1024
        ),
    )(streams_t, hc_proj.T, hc_static, cosr, sinr, rowinfo, keyreq, prefix_group, prefix_t, w_qkv, w_out)
    new_streams = jnp.transpose(new_t, (1, 0, 2))
    suffix_kv = jnp.transpose(kv.reshape(NB, NH, BR, 2, HD), (0, 2, 3, 1, 4)).reshape(R, 2, W)
    return new_streams, suffix_kv


def solution(mesh):
    in_specs = (
        P("tok", None, "head"),
        P(),
        P("head", None),
        P(None, None, "head"),
        P("head", None),
        P("tok", None, "head"),
        P(),
        P(),
        P(),
    )
    out_specs = (P("tok", None, "head"), P("tok", None, "head"))
    return jax.shard_map(shards, mesh=mesh, in_specs=in_specs, out_specs=out_specs, check_vma=False)
```

```python
import functools

import jax
import jax.numpy as jnp
import numpy as np
from jax import lax
from jax.experimental import pallas as pl
from jax.experimental.pallas import tpu as pltpu
from jax.sharding import PartitionSpec as P

HD = 128
STREAMS = 4
GROUPS = 4
COLS = STREAMS + 2
MOST = 1536
BR = 128
PG = 8

EPSILON = 1e-05
MASKED = -1e30
ROPE_BASE = 10000.0
LOG2E = 1.4426950408889634
MESH = pl.DeviceIdType.MESH
NT = (((1,), (1,)), ((), ()))


def remote(src, dst, send_sem, recv_sem, axis, target):
    return pltpu.make_async_remote_copy(
        src_ref=src,
        dst_ref=dst,
        send_sem=send_sem,
        recv_sem=recv_sem,
        device_id={axis: target},
        device_id_type=MESH,
    )


def kernel(
    T, H, R, W, D, NR, PRE,
    streams, hct, hstat, freq, lengths, reqgrp, prefgrp, pk, pv, wqkv_hbm, wout_hbm,
    out, k_out, v_out,
    wqkv, wout, stat, stat_in, ctr, coef, inf, inft, keyreq, pown, cosb, sinb, mix, nrm, qb, kvb, snd_kv, snd_q, pb, psnd,
    mb, lb, acc, ob, om, upd, part, pair_out, pair_in, y_out, y_in,
    w_sem, stat_ss, stat_rs, mix_ys, mix_yr, mix_cs, mix_cr, pz_up, pz_dn, pp_s, p_r, ms_kv, ms_q, q_r, kz_s, k_r,
    o_s, o_r, ro_cs, ro_cr, ro_ys, ro_yr,
):
    NB = R // BR
    C = 2 * NB
    NL = W // HD // 2
    W2 = W // 2
    Y = H // 2
    NP = T // 2
    i = lax.axis_index("tok")
    h = lax.axis_index("head")
    core = lax.rem(h, 2)
    yy = h // 2
    other = h + 1 - 2 * core
    odd = lax.rem(i, 2)
    mate = i + 1 - 2 * odd
    has_up = i + 2 < T
    has_dn = i >= 2
    has_far = i >= 4
    relays = jnp.logical_and(has_up, has_dn)
    scaling = HD ** (-0.5) * LOG2E

    w_copy = pltpu.make_async_copy(wqkv_hbm, wqkv, w_sem.at[0])
    w_copy.start()
    wo_copy = pltpu.make_async_copy(wout_hbm, wout, w_sem.at[1])
    wo_copy.start()
    barrier = pltpu.get_barrier_semaphore()
    for k in range(1, H):
        pl.semaphore_signal(barrier, inc=1, device_id={"head": lax.rem(h + k, H)}, device_id_type=MESH)
    pl.semaphore_signal(barrier, inc=1, device_id={"tok": mate}, device_id_type=MESH)

    @pl.when(has_up)
    def _():
        pl.semaphore_signal(barrier, inc=1, device_id={"tok": i + 2}, device_id_type=MESH)

    @pl.when(has_dn)
    def _():
        pl.semaphore_signal(barrier, inc=1, device_id={"tok": i - 2}, device_id_type=MESH)

    def to_own(lower, upper):
        return jnp.where(odd == 1, upper, lower), jnp.where(odd == 1, lower, upper)

    k_loc, k_oth = to_own(pk[:, 0:W2].astype(jnp.float32), pk[:, W2:W].astype(jnp.float32))
    v_loc, v_oth = to_own(pv[:, 0:W2].astype(jnp.float32), pv[:, W2:W].astype(jnp.float32))
    pb[i, :, 0:W2] = k_loc.astype(jnp.bfloat16)
    pb[i, :, W2:W] = v_loc.astype(jnp.bfloat16)
    psnd[:, 0:W2] = k_oth.astype(jnp.bfloat16)
    psnd[:, W2:W] = v_oth.astype(jnp.bfloat16)

    pl.semaphore_wait(barrier, H + has_up.astype(jnp.int32) + has_dn.astype(jnp.int32))

    def pre_up(b):
        return remote(pb.at[b], pb.at[b], pz_up.at[b], p_r.at[b], "tok", i + 2)

    def pre_dn(b):
        return remote(pb.at[b], pb.at[b], pz_dn.at[b], p_r.at[b], "tok", i - 2)

    def pre_mate():
        return remote(psnd, pb.at[i], pp_s.at[0], p_r.at[i], "tok", mate)

    def pre_got(b):
        remote(psnd, pb.at[b], pp_s.at[0], p_r.at[b], "tok", mate).wait_recv()

    def pre_spread(b):
        @pl.when(has_up)
        def _():
            pre_up(b).start()

        @pl.when(has_dn)
        def _():
            pre_dn(b).start()

    pre_mate().start()
    pre_spread(i)
    STEPS = NP - 1
    first_of = i - odd

    def pre_step(s):
        for e in range(2):
            below = first_of - 2 * s + e
            above = first_of + 2 * s + e

            @pl.when(below >= 0)
            def _():
                pre_got(below)

                @pl.when(has_up)
                def _():
                    pre_up(below).start()

            @pl.when(above < T)
            def _():
                pre_got(above)

                @pl.when(has_dn)
                def _():
                    pre_dn(above).start()

    ones_rows = jnp.ones((16, W), jnp.bfloat16)
    row_id = lax.broadcasted_iota(jnp.int32, (8, R), 0)
    base = hct[...]
    for j in range(STREAMS):
        s = streams[j]
        sf = s.astype(jnp.float32)
        sq = sf * sf
        hi = sq.astype(jnp.bfloat16)
        lo = (sq - hi.astype(jnp.float32)).astype(jnp.bfloat16)
        pr = lax.dot_general(base, s, NT, preferred_element_type=jnp.float32)
        sums = lax.dot_general(ones_rows, s, NT, preferred_element_type=jnp.float32)
        sqs = lax.dot_general(ones_rows, hi, NT, preferred_element_type=jnp.float32) + lax.dot_general(
            ones_rows, lo, NT, preferred_element_type=jnp.float32
        )
        stat[8 * j : 8 * j + 8, :] = jnp.where(row_id == 7, sqs[0:8], sums[0:8])
        stat[8 * j : 8 * j + COLS, :] = pr
    cs = lax.dot_general(base, jnp.ones((R, W), jnp.bfloat16), NT, preferred_element_type=jnp.float32)
    stat[32:40, :] = jnp.zeros((8, R), jnp.float32)
    stat[32 : 32 + COLS, :] = cs

    def stat_copy(k):
        return remote(stat, stat_in.at[k - 1], stat_ss.at[k - 1], stat_rs.at[k - 1], "head", lax.rem(h + k, H))

    for k in range(1, H):
        stat_copy(k).start()

    pos = first_of * R + lax.broadcasted_iota(jnp.int32, (8, 2 * R), 1) - lax.broadcasted_iota(
        jnp.int32, (8, 2 * R), 0
    ) * (2 * R)
    request = jnp.zeros((8, 2 * R), jnp.int32)
    begin = jnp.zeros((8, 2 * R), jnp.int32)
    group = jnp.full((8, 2 * R), reqgrp[0], jnp.int32)
    finish = jnp.int32(0)
    for q in range(NR):
        finish = finish + lengths[q]
        past = finish <= pos
        request = request + past.astype(jnp.int32)
        begin = jnp.where(past, finish, begin)
        group = jnp.where(past, reqgrp[min(q + 1, NR - 1)], group)
    keyreq[...] = request.astype(jnp.float32)
    sub = lax.broadcasted_iota(jnp.int32, (8, 2 * R), 0)
    inf[...] = jnp.zeros_like(inf)
    for row, values in enumerate((request, group, PRE + pos - begin)):
        inf[8 * row : 8 * row + 8, :] = jnp.where(sub == 0, values, 0).astype(jnp.float32)
    inft[...] = jnp.transpose(inf[...])
    for b in range(T):
        pown[:, b * BR : (b + 1) * BR] = jnp.full((8, BR), prefgrp[b], jnp.int32).astype(jnp.float32)
    first_half = lax.broadcasted_iota(jnp.int32, (BR, HD), 1) < HD // 2
    for r in range(NB):
        rows = slice(r * BR, (r + 1) * BR)
        at = pl.ds(pl.multiple_of(odd * R + r * BR, BR), BR)
        angle = inft[at, 16:17] * freq[0:1, :]
        cosb[rows, :] = jnp.cos(angle)
        sine = jnp.sin(angle)
        sinb[rows, :] = jnp.where(first_half, -sine, sine)

    for k in range(1, H):
        stat_copy(k).wait_recv()
    pre_got(mate)
    pre_spread(mate)
    total = stat[...]
    for k in range(1, H):
        total = total + stat_in[k - 1]
    ctr[...] = jnp.zeros_like(ctr)
    col_sum = total[32:40]
    for j in range(STREAMS):
        blk = total[8 * j : 8 * j + 8]
        average = blk[6:7] / D
        spread = blk[7:8] / D - average * average
        inv = lax.rsqrt(spread + EPSILON)
        static = jnp.zeros((8, R), jnp.float32)
        for c in range(COLS):
            static = jnp.where(row_id == c, hstat[j, c], static)
        ctr[8 * j : 8 * j + 8, :] = jnp.tanh((blk - average * col_sum) * inv) + static
    coef[...] = jnp.transpose(ctr[...])

    def mix_y(r, k):
        to = lax.rem(yy + k, Y) * 2 + core
        return remote(mix.at[r, h], mix.at[r, h], mix_ys.at[r, k - 1], mix_yr.at[r, k - 1], "head", to)

    def mix_core(r, k):
        piece = lax.rem(yy + Y - k, Y) * 2 + core
        return remote(mix.at[r, piece], mix.at[r, piece], mix_cs.at[r, k], mix_cr.at[r, k], "head", other)

    for r in range(NB):
        rows = slice(r * BR, (r + 1) * BR)
        total_mix = None
        for j in range(STREAMS):
            term = coef[rows, 8 * j : 8 * j + 1] * streams[j, rows, :].astype(jnp.float32)
            total_mix = term if total_mix is None else total_mix + term
        mix[r, h] = total_mix.astype(jnp.bfloat16)
        for k in range(1, Y):
            mix_y(r, k).start()
        mix_core(r, 0).start()

    def own_share(r):
        rows = slice(r * BR, (r + 1) * BR)
        for q in range(STREAMS):
            share = None
            for j in range(STREAMS):
                term = coef[rows, 8 * j + 1 + q : 8 * j + 2 + q] * streams[j, rows, :].astype(jnp.float32)
                share = term if share is None else share + term
            upd[q, rows, :] = share

    own_share(0)
    next_step = 1
    if next_step <= STEPS:
        pre_step(next_step)
        next_step += 1

    mine = odd * NB
    theirs = (1 - odd) * NB

    def kv_mate(r):
        return remote(snd_kv.at[r], kvb.at[0, mine + r], ms_kv.at[r], k_r.at[0, mine + r], "tok", mate)

    def q_mate(r):
        return remote(snd_q.at[r], qb.at[mine + r], ms_q.at[r], q_r.at[mine + r], "tok", mate)

    def kv_got(level, c):
        remote(snd_kv.at[0], kvb.at[level, c], ms_kv.at[0], k_r.at[level, c], "tok", mate).wait_recv()

    def q_got(c):
        remote(snd_q.at[0], qb.at[c], ms_q.at[0], q_r.at[c], "tok", mate).wait_recv()

    def kv_up(level, c):
        return remote(kvb.at[level, c], kvb.at[level + 1, c], kz_s.at[level, c], k_r.at[level + 1, c], "tok", i + 2)

    def forward(r):
        kv_got(0, theirs + r)

        @pl.when(has_up)
        def _():
            kv_up(0, theirs + r).start()

    for r in range(NB):
        rows = slice(r * BR, (r + 1) * BR)
        for k in range(1, Y):
            mix_y(r, k).wait_recv()
            mix_core(r, k).start()
        for k in range(Y):
            mix_core(r, k).wait_recv()
        if r == 0:
            w_copy.wait()
        summed = None
        for p in range(H):
            piece = jnp.sum(mix[r, p].astype(jnp.float32), -1, keepdims=True)
            summed = piece if summed is None else summed + piece
        center = summed / D
        squares = None
        for p in range(H):
            dev = mix[r, p].astype(jnp.float32) - center
            piece = jnp.sum(dev * dev, -1, keepdims=True)
            squares = piece if squares is None else squares + piece
        inv = lax.rsqrt(squares / D + EPSILON)
        for p in range(H):
            nrm[:, p * W : (p + 1) * W] = ((mix[r, p].astype(jnp.float32) - center) * inv).astype(jnp.bfloat16)
        c = cosb[rows, :]
        sn = sinb[rows, :]

        def rotated(values):
            parts = []
            for n in range(2 * NL):
                one = values[:, n * HD : (n + 1) * HD]
                parts.append(one * c + pltpu.roll(one, HD // 2, 1) * sn)
            return jnp.concatenate(parts, 1)

        kk = rotated(jnp.dot(nrm[...], wqkv[1], preferred_element_type=jnp.float32))
        vv = jnp.dot(nrm[...], wqkv[2], preferred_element_type=jnp.float32)
        k_loc, k_oth = to_own(kk[:, 0:W2], kk[:, W2:W])
        v_loc, v_oth = to_own(vv[:, 0:W2], vv[:, W2:W])
        snd_kv[r, :, 0:W2] = k_oth.astype(jnp.bfloat16)
        snd_kv[r, :, W2:W] = v_oth.astype(jnp.bfloat16)
        kv_mate(r).start()
        kvb[0, mine + r, :, 0:W2] = k_loc.astype(jnp.bfloat16)
        kvb[0, mine + r, :, W2:W] = v_loc.astype(jnp.bfloat16)

        @pl.when(has_up)
        def _():
            kv_up(0, mine + r).start()

        k_out[rows, :] = kk.astype(jnp.bfloat16)
        v_out[rows, :] = vv.astype(jnp.bfloat16)
        qq = rotated(jnp.dot(nrm[...], wqkv[0], preferred_element_type=jnp.float32))
        q_loc, q_oth = to_own(qq[:, 0:W2], qq[:, W2:W])
        snd_q[r] = q_oth.astype(jnp.bfloat16)
        q_mate(r).start()
        qb[mine + r] = q_loc.astype(jnp.bfloat16)
        if r > 0:
            forward(r - 1)
        if next_step <= STEPS:
            pre_step(next_step)
            next_step += 1
    while next_step <= STEPS:
        pre_step(next_step)
        next_step += 1

    def step(n, c, scores, values, first):
        top = jnp.max(scores, 1, keepdims=True)
        if first:
            new_max = top
        else:
            old = mb[n, c][:, 0:1]
            new_max = jnp.maximum(old, top)
        weights = jnp.exp2(scores - new_max)
        count = jnp.sum(weights, 1, keepdims=True)
        numer = jnp.dot(weights.astype(jnp.bfloat16), values, preferred_element_type=jnp.float32)
        if not first:
            scale = jnp.exp2(old - new_max)
            count = count + lb[n, c][:, 0:1] * scale
            numer = numer + acc[n, c] * scale
        mb[n, c] = jnp.broadcast_to(new_max, (BR, HD))
        lb[n, c] = jnp.broadcast_to(count, (BR, HD))
        acc[n, c] = numer

    def row_info(c, column):
        return inft[pl.ds(pl.multiple_of(c * BR, BR), BR), column : column + 1]

    def attend(c, keys, allowed, first):
        size = allowed.shape[1]
        for n in range(NL):
            key = keys[:, :, n * HD : (n + 1) * HD].reshape(size, HD)
            value = keys[:, :, W2 + n * HD : W2 + (n + 1) * HD].reshape(size, HD)
            query = qb[c, :, n * HD : (n + 1) * HD]
            scores = lax.dot_general(query, key, NT, preferred_element_type=jnp.float32) * scaling
            step(n, c, jnp.where(allowed, scores, MASKED), value, first)

    def absorb_prefix(c):
        for g in range((T + PG - 1) // PG):
            lo, hi = g * PG, min(T, (g + 1) * PG)
            allowed = row_info(c, 8) == pown[0:1, lo * BR : hi * BR]
            attend(c, pb.at[lo:hi], allowed, g == 0)

    def absorb(level, c, lo, hi):
        allowed = row_info(c, 0) == keyreq[level : level + 1, lo * BR : hi * BR]
        if level == 0:
            causal = lax.broadcasted_iota(jnp.int32, (BR, (hi - lo) * BR), 1) <= lax.broadcasted_iota(
                jnp.int32, (BR, (hi - lo) * BR), 0
            ) + (c - lo) * BR
            allowed = jnp.logical_and(allowed, causal)
        attend(c, kvb.at[level, lo:hi], allowed, False)

    def over_all(body, lo, hi):
        def one(c, carry):
            body(c)
            return carry

        lax.fori_loop(lo, hi, one, 0)

    forward(NB - 1)
    for r in range(NB):
        q_got(theirs + r)

    order = list(range(C - 1, -1, -1))

    def relay(c):
        @pl.when(has_dn)
        def _():
            kv_got(1, c)

            @pl.when(has_up)
            def _():
                kv_up(1, c).start()

    over_all(absorb_prefix, 0, C)
    for c in range(C):
        absorb(0, c, 0, c + 1)
        if c >= C // 2:
            relay(order[2 * (c - C // 2)])
            relay(order[2 * (c - C // 2) + 1])
    for r in range(1, NB):
        own_share(r)

    @pl.when(has_dn)
    def _():
        over_all(lambda c: absorb(1, c, 0, C), 0, C)

    wo_copy.wait()

    def o_mate(r):
        return remote(ob.at[theirs + r], om.at[r], o_s.at[r], o_r.at[r], "tok", mate)

    def out_core(r):
        return remote(pair_out.at[r], pair_in.at[r], ro_cs.at[r], ro_cr.at[r], "head", other)

    def out_y(r, k):
        to = lax.rem(yy + k, Y)
        return remote(y_out.at[r, k - 1], y_in.at[r, k - 1], ro_ys.at[r, k - 1], ro_yr.at[r, k - 1], "head", to * 2 + core)

    own_rows = pl.ds(pl.multiple_of(odd * W2, HD), W2)
    mate_rows = pl.ds(pl.multiple_of((1 - odd) * W2, HD), W2)

    def finish_heads(c):
        @pl.when(has_far)
        def _():
            kv_got(2, c)
            absorb(2, c, c, C)

        for n in range(NL):
            ob[c, :, n * HD : (n + 1) * HD] = (acc[n, c] / lb[n, c]).astype(jnp.bfloat16)

        @pl.when(odd != c // NB)
        def _():
            o_mate(c % NB).start()

    def project(c):
        r = c % NB

        @pl.when(odd == c // NB)
        def _():
            o_mate(r).wait_recv()
            partial_rows = jnp.dot(ob[c], wout[own_rows, :], preferred_element_type=jnp.float32) + jnp.dot(
                om[r], wout[mate_rows, :], preferred_element_type=jnp.float32
            )
            for p in range(H):
                part[p, r] = partial_rows[:, p * W : (p + 1) * W]
            for q in range(Y):
                pair_out[r, q] = part[2 * q + 1 - core, r].astype(jnp.bfloat16)
            out_core(r).start()

    def pair_sum(c):
        r = c % NB

        @pl.when(odd == c // NB)
        def _():
            out_core(r).wait_recv()
            for k in range(1, Y):
                q = lax.rem(yy + k, Y)
                y_out[r, k - 1] = (part[2 * q + core, r] + pair_in[r, q].astype(jnp.float32)).astype(jnp.bfloat16)
                out_y(r, k).start()

    def update(r):
        rows = slice(r * BR, (r + 1) * BR)
        branch = part[h, r] + pair_in[r, yy].astype(jnp.float32)
        for k in range(1, Y):
            out_y(r, k).wait_recv()
            branch = branch + y_in[r, k - 1].astype(jnp.float32)
        for q in range(STREAMS):
            out[q, rows, :] = (upd[q, rows, :] + coef[rows, 8 * q + 5 : 8 * q + 6] * branch).astype(jnp.bfloat16)

    for at in range(C + 2):
        if at < C:
            finish_heads(order[at])
        if 1 <= at <= C:
            project(order[at - 1])
        if at >= 2:
            pair_sum(order[at - 2])
    for r in reversed(range(NB)):
        update(r)

    for k in range(1, H):
        stat_copy(k).wait_send()
    for r in range(NB):
        for k in range(1, Y):
            mix_y(r, k).wait_send()
        for k in range(Y):
            mix_core(r, k).wait_send()
        kv_mate(r).wait_send()
        q_mate(r).wait_send()
        o_mate(r).wait_send()
        out_core(r).wait_send()
        for k in range(1, Y):
            out_y(r, k).wait_send()

    @pl.when(has_up)
    def _():
        for c in range(C):
            kv_up(0, c).wait_send()

    @pl.when(relays)
    def _():
        for c in range(C):
            kv_up(1, c).wait_send()

    pre_mate().wait_send()

    def spread_done(b, up, down):
        @pl.when(jnp.logical_and(up, has_up))
        def _():
            pre_up(b).wait_send()

        @pl.when(jnp.logical_and(down, has_dn))
        def _():
            pre_dn(b).wait_send()

    for b in range(T):
        spread_done(b, b // 2 <= i // 2, b // 2 >= i // 2)


def shards(streams, hc_static, hc_proj, w_qkv, w_out, prefix_kv, lengths, req_group, prefix_group):
    R = streams.shape[0]
    W = streams.shape[2]
    D = w_qkv.shape[1]
    T = lax.axis_size("tok")
    H = lax.axis_size("head")
    NL = W // HD // 2
    W2 = W // 2
    NB = R // BR
    C = 2 * NB
    Y = H // 2
    assert R % BR == 0 and 4 * R >= MOST and T % 2 == 0 and prefix_kv.shape[0] == BR
    prefix_len = prefix_kv.shape[0] * T // GROUPS
    half = np.arange(HD // 2).astype(np.float32)
    freq = np.float32(ROPE_BASE) ** (-(half * np.float32(2.0) / np.float32(HD)))
    freq = jnp.asarray(np.tile(np.concatenate([freq, freq])[None, :], (8, 1)).astype(np.float32))
    streams_t = jnp.transpose(streams, (1, 0, 2))

    vm = pl.BlockSpec(memory_space=pltpu.VMEM)
    sm = pl.BlockSpec(memory_space=pltpu.SMEM)
    hbm = pl.BlockSpec(memory_space=pl.ANY)
    dma = pltpu.SemaphoreType.DMA
    bf, f32 = jnp.bfloat16, jnp.float32
    new_t, k_new, v_new = pl.pallas_call(
        functools.partial(kernel, T, H, R, W, D, lengths.shape[0], prefix_len),
        out_shape=(
            jax.ShapeDtypeStruct((STREAMS, R, W), bf),
            jax.ShapeDtypeStruct((R, W), bf),
            jax.ShapeDtypeStruct((R, W), bf),
        ),
        in_specs=[vm, vm, sm, vm, sm, sm, sm, vm, vm, hbm, hbm],
        out_specs=(vm, vm, vm),
        scratch_shapes=[
            pltpu.VMEM((3, D, W), bf),
            pltpu.VMEM((W, D), bf),
            pltpu.VMEM((40, R), f32),
            pltpu.VMEM((H - 1, 40, R), f32),
            pltpu.VMEM((128, R), f32),
            pltpu.VMEM((R, 128), f32),
            pltpu.VMEM((128, 2 * R), f32),
            pltpu.VMEM((2 * R, 128), f32),
            pltpu.VMEM((8, 2 * R), f32),
            pltpu.VMEM((8, T * BR), f32),
            pltpu.VMEM((R, HD), f32),
            pltpu.VMEM((R, HD), f32),
            pltpu.VMEM((NB, H, BR, W), bf),
            pltpu.VMEM((BR, D), bf),
            pltpu.VMEM((C, BR, W2), bf),
            pltpu.VMEM((3, C, BR, W), bf),
            pltpu.VMEM((NB, BR, W), bf),
            pltpu.VMEM((NB, BR, W2), bf),
            pltpu.VMEM((T, BR, W), bf),
            pltpu.VMEM((BR, W), bf),
            pltpu.VMEM((NL, C, BR, HD), f32),
            pltpu.VMEM((NL, C, BR, HD), f32),
            pltpu.VMEM((NL, C, BR, HD), f32),
            pltpu.VMEM((C, BR, W2), bf),
            pltpu.VMEM((NB, BR, W2), bf),
            pltpu.VMEM((STREAMS, R, W), f32),
            pltpu.VMEM((H, NB, BR, W), f32),
            pltpu.VMEM((NB, Y, BR, W), bf),
            pltpu.VMEM((NB, Y, BR, W), bf),
            pltpu.VMEM((NB, Y - 1, BR, W), bf),
            pltpu.VMEM((NB, Y - 1, BR, W), bf),
            dma((2,)),
            dma((H - 1,)),
            dma((H - 1,)),
            dma((NB, Y - 1)),
            dma((NB, Y - 1)),
            dma((NB, Y)),
            dma((NB, Y)),
            dma((T,)),
            dma((T,)),
            dma((1,)),
            dma((T,)),
            dma((NB,)),
            dma((NB,)),
            dma((C,)),
            dma((2, C)),
            dma((3, C)),
            dma((NB,)),
            dma((NB,)),
            dma((NB,)),
            dma((NB,)),
            dma((NB, Y - 1)),
            dma((NB, Y - 1)),
        ],
        compiler_params=pltpu.CompilerParams(
            collective_id=0, has_side_effects=True, vmem_limit_bytes=56 * 1024 * 1024
        ),
    )(
        streams_t, hc_proj.T, hc_static, freq, lengths, req_group, prefix_group,
        prefix_kv[:, 0, :], prefix_kv[:, 1, :], w_qkv, w_out,
    )
    return jnp.transpose(new_t, (1, 0, 2)), jnp.stack([k_new, v_new], 1)


def solution(mesh):
    in_specs = (
        P("tok", None, "head"),
        P(),
        P("head", None),
        P(None, None, "head"),
        P("head", None),
        P("tok", None, "head"),
        P(),
        P(),
        P(),
    )
    out_specs = (P("tok", None, "head"), P("tok", None, "head"))
    return jax.shard_map(shards, mesh=mesh, in_specs=in_specs, out_specs=out_specs, check_vma=False)
```

```python
import functools

import jax
import jax.numpy as jnp
import numpy as np
from jax import lax
from jax.experimental import pallas as pl
from jax.experimental.pallas import tpu as pltpu
from jax.sharding import PartitionSpec as P

HD = 128
STREAMS = 4
GROUPS = 4
COLS = STREAMS + 2
MOST = 1536
BR = 128
PG = 8

EPSILON = 1e-05
MASKED = -1e30
ROPE_BASE = 10000.0
LOG2E = 1.4426950408889634
MESH = pl.DeviceIdType.MESH
NT = (((1,), (1,)), ((), ()))


def remote(src, dst, send_sem, recv_sem, axis, target):
    return pltpu.make_async_remote_copy(
        src_ref=src,
        dst_ref=dst,
        send_sem=send_sem,
        recv_sem=recv_sem,
        device_id={axis: target},
        device_id_type=MESH,
    )


def kernel(
    T, H, R, W, D, NR, PRE,
    streams, hct, hstat, freq, lengths, reqgrp, prefgrp, pt, wqkv_hbm, wout_hbm,
    out, k_out, v_out,
    wqkv, wout, stat, stat_in, ctr, coef, inf, inft, keyreq, pown, cosb, sinb, mix, nrm, qb, kvb, snd_kv, snd_q, qd, pb,
    mb, lb, acc, part_o, part_s, got_o, got_s, ob, om, upd, part, pair_out, pair_in, y_out, y_in,
    w_sem, stat_ss, stat_rs, mix_ys, mix_yr, mix_cs, mix_cr, pz_up, pz_dn, pp_s, p_r, ms_kv, ms_q, q_r, kz_s, k_r, qd_s, qd_r, po_s, po_r, ps_s, ps_r,
    o_s, o_r, ro_cs, ro_cr, ro_ys, ro_yr,
):
    NB = R // BR
    C = 2 * NB
    NL = W // HD // 2
    W2 = W // 2
    Y = H // 2
    NP = T // 2
    i = lax.axis_index("tok")
    h = lax.axis_index("head")
    core = lax.rem(h, 2)
    yy = h // 2
    other = h + 1 - 2 * core
    odd = lax.rem(i, 2)
    mate = i + 1 - 2 * odd
    has_up = i + 2 < T
    has_dn = i >= 2
    has_far = i >= 4
    helps = jnp.logical_and(has_up, has_dn)
    scaling = HD ** (-0.5) * LOG2E

    w_copy = pltpu.make_async_copy(wqkv_hbm, wqkv, w_sem.at[0])
    w_copy.start()
    wo_copy = pltpu.make_async_copy(wout_hbm, wout, w_sem.at[1])
    wo_copy.start()
    barrier = pltpu.get_barrier_semaphore()
    for k in range(1, H):
        pl.semaphore_signal(barrier, inc=1, device_id={"head": lax.rem(h + k, H)}, device_id_type=MESH)
    pl.semaphore_signal(barrier, inc=1, device_id={"tok": mate}, device_id_type=MESH)

    @pl.when(has_up)
    def _():
        pl.semaphore_signal(barrier, inc=1, device_id={"tok": i + 2}, device_id_type=MESH)

    @pl.when(has_dn)
    def _():
        pl.semaphore_signal(barrier, inc=1, device_id={"tok": i - 2}, device_id_type=MESH)

    def to_own(lower, upper):
        return jnp.where(odd == 1, upper, lower), jnp.where(odd == 1, lower, upper)

    own_heads = pl.ds(odd * NL, NL)
    mate_heads = pl.ds((1 - odd) * NL, NL)
    pb[i] = pt[own_heads]
    pl.semaphore_wait(barrier, H + has_up.astype(jnp.int32) + has_dn.astype(jnp.int32))

    def pre_up(b):
        return remote(pb.at[b], pb.at[b], pz_up.at[b], p_r.at[b], "tok", i + 2)

    def pre_dn(b):
        return remote(pb.at[b], pb.at[b], pz_dn.at[b], p_r.at[b], "tok", i - 2)

    def pre_mate():
        return remote(pt.at[mate_heads], pb.at[i], pp_s.at[0], p_r.at[i], "tok", mate)

    def pre_got(b):
        remote(pt.at[mate_heads], pb.at[b], pp_s.at[0], p_r.at[b], "tok", mate).wait_recv()

    def pre_spread(b):
        @pl.when(has_up)
        def _():
            pre_up(b).start()

        @pl.when(has_dn)
        def _():
            pre_dn(b).start()

    pre_mate().start()
    pre_spread(i)
    STEPS = NP - 1
    first_of = i - odd

    def pre_step(s):
        for e in range(2):
            below = first_of - 2 * s + e
            above = first_of + 2 * s + e

            @pl.when(below >= 0)
            def _():
                pre_got(below)

                @pl.when(has_up)
                def _():
                    pre_up(below).start()

            @pl.when(above < T)
            def _():
                pre_got(above)

                @pl.when(has_dn)
                def _():
                    pre_dn(above).start()

    ones_rows = jnp.ones((16, W), jnp.bfloat16)
    row_id = lax.broadcasted_iota(jnp.int32, (8, R), 0)
    base = hct[...]
    for j in range(STREAMS):
        s = streams[j]
        sf = s.astype(jnp.float32)
        sq = sf * sf
        hi = sq.astype(jnp.bfloat16)
        lo = (sq - hi.astype(jnp.float32)).astype(jnp.bfloat16)
        pr = lax.dot_general(base, s, NT, preferred_element_type=jnp.float32)
        sums = lax.dot_general(ones_rows, s, NT, preferred_element_type=jnp.float32)
        sqs = lax.dot_general(ones_rows, hi, NT, preferred_element_type=jnp.float32) + lax.dot_general(
            ones_rows, lo, NT, preferred_element_type=jnp.float32
        )
        stat[8 * j : 8 * j + 8, :] = jnp.where(row_id == 7, sqs[0:8], sums[0:8])
        stat[8 * j : 8 * j + COLS, :] = pr
    cs = lax.dot_general(base, jnp.ones((R, W), jnp.bfloat16), NT, preferred_element_type=jnp.float32)
    stat[32:40, :] = jnp.zeros((8, R), jnp.float32)
    stat[32 : 32 + COLS, :] = cs

    def stat_copy(k):
        return remote(stat, stat_in.at[k - 1], stat_ss.at[k - 1], stat_rs.at[k - 1], "head", lax.rem(h + k, H))

    for k in range(1, H):
        stat_copy(k).start()

    sub = lax.broadcasted_iota(jnp.int32, (8, 2 * R), 0)
    pos = first_of * R + lax.broadcasted_iota(jnp.int32, (8, 2 * R), 1) + (1 - sub) * (2 * R)
    request = jnp.zeros((8, 2 * R), jnp.int32)
    begin = jnp.zeros((8, 2 * R), jnp.int32)
    group = jnp.full((8, 2 * R), reqgrp[0], jnp.int32)
    finish = jnp.int32(0)
    for q in range(NR):
        finish = finish + lengths[q]
        past = finish <= pos
        request = request + past.astype(jnp.int32)
        begin = jnp.where(past, finish, begin)
        group = jnp.where(past, reqgrp[min(q + 1, NR - 1)], group)
    keyreq[...] = request.astype(jnp.float32)
    inf[...] = jnp.zeros_like(inf)
    for row, values in enumerate((request, group, PRE + pos - begin)):
        inf[8 * row : 8 * row + 8, :] = jnp.where(sub <= 1, values, 0).astype(jnp.float32)
    inft[...] = jnp.transpose(inf[...])
    for b in range(T):
        pown[:, b * BR : (b + 1) * BR] = jnp.full((8, BR), prefgrp[b], jnp.int32).astype(jnp.float32)
    first_half = lax.broadcasted_iota(jnp.int32, (BR, HD), 1) < HD // 2
    for r in range(NB):
        rows = slice(r * BR, (r + 1) * BR)
        at = pl.ds(pl.multiple_of(odd * R + r * BR, BR), BR)
        angle = inft[at, 17:18] * freq[0:1, :]
        cosb[rows, :] = jnp.cos(angle)
        sine = jnp.sin(angle)
        sinb[rows, :] = jnp.where(first_half, -sine, sine)

    pre_got(mate)
    pre_spread(mate)
    for k in range(1, H):
        stat_copy(k).wait_recv()
    total = stat[...]
    for k in range(1, H):
        total = total + stat_in[k - 1]
    ctr[...] = jnp.zeros_like(ctr)
    col_sum = total[32:40]
    for j in range(STREAMS):
        blk = total[8 * j : 8 * j + 8]
        average = blk[6:7] / D
        spread = blk[7:8] / D - average * average
        inv = lax.rsqrt(spread + EPSILON)
        static = jnp.zeros((8, R), jnp.float32)
        for c in range(COLS):
            static = jnp.where(row_id == c, hstat[j, c], static)
        ctr[8 * j : 8 * j + 8, :] = jnp.tanh((blk - average * col_sum) * inv) + static
    coef[...] = jnp.transpose(ctr[...])

    def mix_y(r, k):
        to = lax.rem(yy + k, Y) * 2 + core
        return remote(mix.at[r, h], mix.at[r, h], mix_ys.at[r, k - 1], mix_yr.at[r, k - 1], "head", to)

    def mix_core(r, k):
        piece = lax.rem(yy + Y - k, Y) * 2 + core
        return remote(mix.at[r, piece], mix.at[r, piece], mix_cs.at[r, k], mix_cr.at[r, k], "head", other)

    for r in range(NB):
        rows = slice(r * BR, (r + 1) * BR)
        total_mix = None
        for j in range(STREAMS):
            term = coef[rows, 8 * j : 8 * j + 1] * streams[j, rows, :].astype(jnp.float32)
            total_mix = term if total_mix is None else total_mix + term
        mix[r, h] = total_mix.astype(jnp.bfloat16)
        for k in range(1, Y):
            mix_y(r, k).start()
        mix_core(r, 0).start()

    def own_share(r):
        rows = slice(r * BR, (r + 1) * BR)
        for q in range(STREAMS):
            share = None
            for j in range(STREAMS):
                term = coef[rows, 8 * j + 1 + q : 8 * j + 2 + q] * streams[j, rows, :].astype(jnp.float32)
                share = term if share is None else share + term
            upd[q, rows, :] = share

    own_share(0)
    next_step = 1
    if next_step <= STEPS:
        pre_step(next_step)
        next_step += 1

    mine = odd * NB
    theirs = (1 - odd) * NB

    def kv_mate(r):
        return remote(snd_kv.at[r], kvb.at[0, mine + r], ms_kv.at[r], k_r.at[0, mine + r], "tok", mate)

    def q_mate(r):
        return remote(snd_q.at[r], qb.at[mine + r], ms_q.at[r], q_r.at[mine + r], "tok", mate)

    def kv_got(level, c):
        remote(snd_kv.at[0], kvb.at[level, c], ms_kv.at[0], k_r.at[level, c], "tok", mate).wait_recv()

    def q_got(c):
        remote(snd_q.at[0], qb.at[c], ms_q.at[0], q_r.at[c], "tok", mate).wait_recv()

    def kv_up(level, c):
        return remote(kvb.at[level, c], kvb.at[level + 1, c], kz_s.at[level, c], k_r.at[level + 1, c], "tok", i + 2)

    def q_down(c):
        return remote(qb.at[c], qd.at[c], qd_s.at[c], qd_r.at[c], "tok", i - 2)

    def forward_kv(r):
        kv_got(0, theirs + r)

        @pl.when(has_up)
        def _():
            kv_up(0, theirs + r).start()

    def forward_q(r):
        q_got(theirs + r)

        @pl.when(has_far)
        def _():
            q_down(theirs + r).start()

    for r in range(NB):
        rows = slice(r * BR, (r + 1) * BR)
        for k in range(1, Y):
            mix_y(r, k).wait_recv()
            mix_core(r, k).start()
        for k in range(Y):
            mix_core(r, k).wait_recv()
        if r == 0:
            w_copy.wait()
        summed = None
        for p in range(H):
            piece = jnp.sum(mix[r, p].astype(jnp.float32), -1, keepdims=True)
            summed = piece if summed is None else summed + piece
        center = summed / D
        squares = None
        for p in range(H):
            dev = mix[r, p].astype(jnp.float32) - center
            piece = jnp.sum(dev * dev, -1, keepdims=True)
            squares = piece if squares is None else squares + piece
        inv = lax.rsqrt(squares / D + EPSILON)
        for p in range(H):
            nrm[:, p * W : (p + 1) * W] = ((mix[r, p].astype(jnp.float32) - center) * inv).astype(jnp.bfloat16)
        c = cosb[rows, :]
        sn = sinb[rows, :]

        def rotated(values):
            parts = []
            for n in range(2 * NL):
                one = values[:, n * HD : (n + 1) * HD]
                parts.append(one * c + pltpu.roll(one, HD // 2, 1) * sn)
            return jnp.concatenate(parts, 1)

        kk = rotated(jnp.dot(nrm[...], wqkv[1], preferred_element_type=jnp.float32))
        vv = jnp.dot(nrm[...], wqkv[2], preferred_element_type=jnp.float32)
        k_loc, k_oth = to_own(kk[:, 0:W2], kk[:, W2:W])
        v_loc, v_oth = to_own(vv[:, 0:W2], vv[:, W2:W])
        snd_kv[r, :, 0:W2] = k_oth.astype(jnp.bfloat16)
        snd_kv[r, :, W2:W] = v_oth.astype(jnp.bfloat16)
        kv_mate(r).start()
        kvb[0, mine + r, :, 0:W2] = k_loc.astype(jnp.bfloat16)
        kvb[0, mine + r, :, W2:W] = v_loc.astype(jnp.bfloat16)

        @pl.when(has_up)
        def _():
            kv_up(0, mine + r).start()

        k_out[rows, :] = kk.astype(jnp.bfloat16)
        v_out[rows, :] = vv.astype(jnp.bfloat16)
        qq = rotated(jnp.dot(nrm[...], wqkv[0], preferred_element_type=jnp.float32))
        q_loc, q_oth = to_own(qq[:, 0:W2], qq[:, W2:W])
        snd_q[r] = q_oth.astype(jnp.bfloat16)
        q_mate(r).start()
        qb[mine + r] = q_loc.astype(jnp.bfloat16)

        @pl.when(has_far)
        def _():
            q_down(mine + r).start()

        if r > 0:
            forward_kv(r - 1)
        if r > 1:
            forward_q(r - 2)
        if next_step <= STEPS:
            pre_step(next_step)
            next_step += 1
    while next_step <= STEPS:
        pre_step(next_step)
        next_step += 1

    def weigh(query, key, value, allowed, floor):
        scores = lax.dot_general(query, key, NT, preferred_element_type=jnp.float32) * scaling
        scores = jnp.where(allowed, scores, MASKED)
        top = jnp.max(scores, 1, keepdims=True)
        if floor is not None:
            top = jnp.maximum(floor, top)
        weights = jnp.exp2(scores - top)
        count = jnp.sum(weights, 1, keepdims=True)
        return top, count, jnp.dot(weights.astype(jnp.bfloat16), value, preferred_element_type=jnp.float32)

    def keep(n, c, top, count, numer):
        mb[n, c] = jnp.broadcast_to(top, (BR, HD))
        lb[n, c] = jnp.broadcast_to(count, (BR, HD))
        acc[n, c] = numer

    def attend(c, pieces, allowed, first):
        for n in range(NL):
            key, value = pieces(n)
            old = None if first else mb[n, c][:, 0:1]
            top, count, numer = weigh(qb[c, :, n * HD : (n + 1) * HD], key, value, allowed, old)
            if not first:
                scale = jnp.exp2(old - top)
                count = count + lb[n, c][:, 0:1] * scale
                numer = numer + acc[n, c] * scale
            keep(n, c, top, count, numer)

    def row_info(c, column):
        return inft[pl.ds(pl.multiple_of(c * BR, BR), BR), column : column + 1]

    def absorb_prefix(c):
        for g in range((T + PG - 1) // PG):
            lo, hi = g * PG, min(T, (g + 1) * PG)

            def pieces(n):
                kv = pb[lo:hi, n].reshape((hi - lo) * BR, 2 * HD)
                return kv[:, 0:HD], kv[:, HD : 2 * HD]

            attend(c, pieces, row_info(c, 9) == pown[0:1, lo * BR : hi * BR], g == 0)

    def kv_pieces(level, lo, hi):
        def pieces(n):
            size = (hi - lo) * BR
            key = kvb[level, lo:hi, :, n * HD : (n + 1) * HD].reshape(size, HD)
            return key, kvb[level, lo:hi, :, W2 + n * HD : W2 + (n + 1) * HD].reshape(size, HD)

        return pieces

    def absorb(level, c, lo, hi):
        allowed = row_info(c, 1) == keyreq[level + 1 : level + 2, lo * BR : hi * BR]
        if level == 0:
            causal = lax.broadcasted_iota(jnp.int32, (BR, (hi - lo) * BR), 1) <= lax.broadcasted_iota(
                jnp.int32, (BR, (hi - lo) * BR), 0
            ) + (c - lo) * BR
            allowed = jnp.logical_and(allowed, causal)
        attend(c, kv_pieces(level, lo, hi), allowed, False)

    lane = lax.broadcasted_iota(jnp.int32, (BR, HD), 1)

    def part_copies(c):
        return (
            remote(part_o.at[c], got_o.at[c], po_s.at[c], po_r.at[c], "tok", i + 2),
            remote(part_s.at[c], got_s.at[c], ps_s.at[c], ps_r.at[c], "tok", i + 2),
        )

    def help_up(c):
        pieces = kv_pieces(1, c, C)
        allowed = row_info(c, 0) == keyreq[2:3, c * BR : C * BR]
        remote(qb.at[c], qd.at[c], qd_s.at[c], qd_r.at[c], "tok", i + 2).wait_recv()
        sums = jnp.zeros((BR, HD), jnp.float32)
        for n in range(NL):
            key, value = pieces(n)
            top, count, numer = weigh(qd[c, :, n * HD : (n + 1) * HD], key, value, allowed, None)
            part_o[c, :, n * HD : (n + 1) * HD] = (numer / count).astype(jnp.bfloat16)
            sums = jnp.where(lane == n, top, jnp.where(lane == NL + n, count, sums))
        part_s[c] = jnp.transpose(sums)[0:8]
        for copy in part_copies(c):
            copy.start()

    def merge_part(c):
        for copy in part_copies(c):
            copy.wait_recv()
        sums = jnp.transpose(jnp.concatenate([got_s[c], jnp.zeros((HD - 8, BR), jnp.float32)], 0))
        for n in range(NL):
            far_top, far_count = sums[:, n : n + 1], sums[:, NL + n : NL + n + 1]
            old = mb[n, c][:, 0:1]
            top = jnp.maximum(old, far_top)
            scale = jnp.exp2(old - top)
            far = far_count * jnp.exp2(far_top - top)
            lb[n, c] = lb[n, c] * scale + far
            acc[n, c] = acc[n, c] * scale + got_o[c, :, n * HD : (n + 1) * HD].astype(jnp.float32) * far

    def over_all(body, lo, hi):
        def one(c, carry):
            body(c)
            return carry

        lax.fori_loop(lo, hi, one, 0)

    forward_kv(NB - 1)
    for r in range(max(0, NB - 2), NB):
        forward_q(r)

    order = [c for r in reversed(range(NB)) for c in (NB + r, r)]

    over_all(absorb_prefix, 0, C)
    for c in range(C):
        absorb(0, c, 0, c + 1)
    for r in range(1, NB):
        own_share(r)

    @pl.when(has_dn)
    def _():
        for c in range(C):
            kv_got(1, c)

    @pl.when(helps)
    def _():
        for c in order:
            help_up(c)

    wo_copy.wait()

    def o_mate(r):
        return remote(ob.at[theirs + r], om.at[r], o_s.at[r], o_r.at[r], "tok", mate)

    def out_core(r):
        return remote(pair_out.at[r], pair_in.at[r], ro_cs.at[r], ro_cr.at[r], "head", other)

    def out_y(r, k):
        to = lax.rem(yy + k, Y)
        return remote(y_out.at[r, k - 1], y_in.at[r, k - 1], ro_ys.at[r, k - 1], ro_yr.at[r, k - 1], "head", to * 2 + core)

    own_rows = pl.ds(pl.multiple_of(odd * W2, HD), W2)
    mate_rows = pl.ds(pl.multiple_of((1 - odd) * W2, HD), W2)

    def finish_heads(c):
        @pl.when(has_dn)
        def _():
            absorb(1, c, 0, C)

        @pl.when(has_far)
        def _():
            merge_part(c)

        for n in range(NL):
            ob[c, :, n * HD : (n + 1) * HD] = (acc[n, c] / lb[n, c]).astype(jnp.bfloat16)

        @pl.when(odd != c // NB)
        def _():
            o_mate(c % NB).start()

    def project(c):
        r = c % NB

        @pl.when(odd == c // NB)
        def _():
            o_mate(r).wait_recv()
            partial_rows = jnp.dot(ob[c], wout[own_rows, :], preferred_element_type=jnp.float32) + jnp.dot(
                om[r], wout[mate_rows, :], preferred_element_type=jnp.float32
            )
            for p in range(H):
                part[p, r] = partial_rows[:, p * W : (p + 1) * W]
            for q in range(Y):
                pair_out[r, q] = part[2 * q + 1 - core, r].astype(jnp.bfloat16)
            out_core(r).start()

    def pair_sum(c):
        r = c % NB

        @pl.when(odd == c // NB)
        def _():
            out_core(r).wait_recv()
            for k in range(1, Y):
                q = lax.rem(yy + k, Y)
                y_out[r, k - 1] = (part[2 * q + core, r] + pair_in[r, q].astype(jnp.float32)).astype(jnp.bfloat16)
                out_y(r, k).start()

    def update(r):
        rows = slice(r * BR, (r + 1) * BR)
        branch = part[h, r] + pair_in[r, yy].astype(jnp.float32)
        for k in range(1, Y):
            out_y(r, k).wait_recv()
            branch = branch + y_in[r, k - 1].astype(jnp.float32)
        for q in range(STREAMS):
            out[q, rows, :] = (upd[q, rows, :] + coef[rows, 8 * q + 5 : 8 * q + 6] * branch).astype(jnp.bfloat16)

    for at in range(C + 2):
        if at < C:
            finish_heads(order[at])
        if 1 <= at <= C:
            project(order[at - 1])
        if at >= 2:
            pair_sum(order[at - 2])
    for r in reversed(range(NB)):
        update(r)

    for k in range(1, H):
        stat_copy(k).wait_send()
    for r in range(NB):
        for k in range(1, Y):
            mix_y(r, k).wait_send()
        for k in range(Y):
            mix_core(r, k).wait_send()
        kv_mate(r).wait_send()
        q_mate(r).wait_send()
        o_mate(r).wait_send()
        out_core(r).wait_send()
        for k in range(1, Y):
            out_y(r, k).wait_send()

    @pl.when(has_up)
    def _():
        for c in range(C):
            kv_up(0, c).wait_send()

    @pl.when(helps)
    def _():
        for c in range(C):
            for copy in part_copies(c):
                copy.wait_send()

    @pl.when(has_far)
    def _():
        for c in range(C):
            q_down(c).wait_send()

    pre_mate().wait_send()

    def spread_done(b, up, down):
        @pl.when(jnp.logical_and(up, has_up))
        def _():
            pre_up(b).wait_send()

        @pl.when(jnp.logical_and(down, has_dn))
        def _():
            pre_dn(b).wait_send()

    for b in range(T):
        spread_done(b, b // 2 <= i // 2, b // 2 >= i // 2)


def shards(streams, hc_static, hc_proj, w_qkv, w_out, prefix_kv, lengths, req_group, prefix_group):
    R = streams.shape[0]
    W = streams.shape[2]
    D = w_qkv.shape[1]
    T = lax.axis_size("tok")
    H = lax.axis_size("head")
    NL = W // HD // 2
    W2 = W // 2
    NB = R // BR
    C = 2 * NB
    Y = H // 2
    assert R % BR == 0 and 4 * R >= MOST and T % 2 == 0 and prefix_kv.shape[0] == BR
    prefix_len = prefix_kv.shape[0] * T // GROUPS
    half = np.arange(HD // 2).astype(np.float32)
    freq = np.float32(ROPE_BASE) ** (-(half * np.float32(2.0) / np.float32(HD)))
    freq = jnp.asarray(np.tile(np.concatenate([freq, freq])[None, :], (8, 1)).astype(np.float32))
    streams_t = jnp.transpose(streams, (1, 0, 2))
    prefix_t = jnp.transpose(prefix_kv.reshape(BR, 2, 2 * NL, HD), (2, 0, 1, 3)).reshape(2 * NL, BR, 2 * HD)

    vm = pl.BlockSpec(memory_space=pltpu.VMEM)
    sm = pl.BlockSpec(memory_space=pltpu.SMEM)
    hbm = pl.BlockSpec(memory_space=pltpu.HBM)
    dma = pltpu.SemaphoreType.DMA
    bf, f32 = jnp.bfloat16, jnp.float32
    new_t, k_new, v_new = pl.pallas_call(
        functools.partial(kernel, T, H, R, W, D, lengths.shape[0], prefix_len),
        out_shape=(
            pltpu.VMEM((STREAMS, R, W), bf),
            pltpu.VMEM((R, W), bf),
            pltpu.VMEM((R, W), bf),
        ),
        in_specs=[vm, vm, sm, vm, sm, sm, sm, vm, hbm, hbm],
        out_specs=(vm, vm, vm),
        scratch_shapes=[
            pltpu.VMEM((3, D, W), bf),
            pltpu.VMEM((W, D), bf),
            pltpu.VMEM((40, R), f32),
            pltpu.VMEM((H - 1, 40, R), f32),
            pltpu.VMEM((128, R), f32),
            pltpu.VMEM((R, 128), f32),
            pltpu.VMEM((128, 2 * R), f32),
            pltpu.VMEM((2 * R, 128), f32),
            pltpu.VMEM((8, 2 * R), f32),
            pltpu.VMEM((8, T * BR), f32),
            pltpu.VMEM((R, HD), f32),
            pltpu.VMEM((R, HD), f32),
            pltpu.VMEM((NB, H, BR, W), bf),
            pltpu.VMEM((BR, D), bf),
            pltpu.VMEM((C, BR, W2), bf),
            pltpu.VMEM((2, C, BR, W), bf),
            pltpu.VMEM((NB, BR, W), bf),
            pltpu.VMEM((NB, BR, W2), bf),
            pltpu.VMEM((C, BR, W2), bf),
            pltpu.VMEM((T, NL, BR, 2 * HD), bf),
            pltpu.VMEM((NL, C, BR, HD), f32),
            pltpu.VMEM((NL, C, BR, HD), f32),
            pltpu.VMEM((NL, C, BR, HD), f32),
            pltpu.VMEM((C, BR, W2), bf),
            pltpu.VMEM((C, 8, BR), f32),
            pltpu.VMEM((C, BR, W2), bf),
            pltpu.VMEM((C, 8, BR), f32),
            pltpu.VMEM((C, BR, W2), bf),
            pltpu.VMEM((NB, BR, W2), bf),
            pltpu.VMEM((STREAMS, R, W), f32),
            pltpu.VMEM((H, NB, BR, W), f32),
            pltpu.VMEM((NB, Y, BR, W), bf),
            pltpu.VMEM((NB, Y, BR, W), bf),
            pltpu.VMEM((NB, Y - 1, BR, W), bf),
            pltpu.VMEM((NB, Y - 1, BR, W), bf),
            dma((2,)),
            dma((H - 1,)),
            dma((H - 1,)),
            dma((NB, Y - 1)),
            dma((NB, Y - 1)),
            dma((NB, Y)),
            dma((NB, Y)),
            dma((T,)),
            dma((T,)),
            dma((1,)),
            dma((T,)),
            dma((NB,)),
            dma((NB,)),
            dma((C,)),
            dma((1, C)),
            dma((2, C)),
            dma((C,)),
            dma((C,)),
            dma((C,)),
            dma((C,)),
            dma((C,)),
            dma((C,)),
            dma((NB,)),
            dma((NB,)),
            dma((NB,)),
            dma((NB,)),
            dma((NB, Y - 1)),
            dma((NB, Y - 1)),
        ],
        compiler_params=pltpu.CompilerParams(
            collective_id=0, has_side_effects=True, vmem_limit_bytes=44 * 1024 * 1024
        ),
    )(
        streams_t, hc_proj.T, hc_static, freq, lengths, req_group, prefix_group,
        prefix_t, w_qkv, w_out,
    )
    return jnp.transpose(new_t, (1, 0, 2)), jnp.stack([k_new, v_new], 1)


def solution(mesh):
    in_specs = (
        P("tok", None, "head"),
        P(),
        P("head", None),
        P(None, None, "head"),
        P("head", None),
        P("tok", None, "head"),
        P(),
        P(),
        P(),
    )
    out_specs = (P("tok", None, "head"), P("tok", None, "head"))
    return jax.shard_map(shards, mesh=mesh, in_specs=in_specs, out_specs=out_specs, check_vma=False)
```

```python
import functools

import jax
import jax.numpy as jnp
import numpy as np
from jax import lax
from jax.experimental import pallas as pl
from jax.experimental.pallas import tpu as pltpu
from jax.sharding import PartitionSpec as P

HD = 128
STREAMS = 4
GROUPS = 4
COLS = STREAMS + 2
MOST = 1536
BR = 128
PG = 8

EPSILON = 1e-05
MASKED = -1e30
ROPE_BASE = 10000.0
LOG2E = 1.4426950408889634
MESH = pl.DeviceIdType.MESH
NT = (((1,), (1,)), ((), ()))


def remote(src, dst, send_sem, recv_sem, axis, target):
    return pltpu.make_async_remote_copy(
        src_ref=src,
        dst_ref=dst,
        send_sem=send_sem,
        recv_sem=recv_sem,
        device_id={axis: target},
        device_id_type=MESH,
    )


def kernel(
    T, H, R, W, D, NR, PRE,
    streams, hct, hstat, freq, lengths, reqgrp, prefgrp, pt, wqkv_hbm, wout_hbm,
    out, k_out, v_out,
    wqkv, wout, stat, stat_in, ctr, coef, inf, inft, keyreq, pown, cosb, sinb, mix, nrm, qb, kvb, snd_kv, snd_q, qd, pb,
    mb, lb, acc, part_o, part_s, got_o, got_s, ob, om, upd, part, pair_out, pair_in, y_out, y_in,
    w_sem, stat_ss, stat_rs, mix_ys, mix_yr, mix_cs, mix_cr, pz_up, pz_dn, pp_s, p_r, ms_kv, ms_q, q_r, kz_s, k_r, qd_s, qd_r, po_s, po_r, ps_s, ps_r,
    o_s, o_r, ro_cs, ro_cr, ro_ys, ro_yr,
):
    NB = R // BR
    C = 2 * NB
    NL = W // HD // 2
    W2 = W // 2
    Y = H // 2
    NP = T // 2
    i = lax.axis_index("tok")
    h = lax.axis_index("head")
    core = lax.rem(h, 2)
    yy = h // 2
    other = h + 1 - 2 * core
    odd = lax.rem(i, 2)
    mate = i + 1 - 2 * odd
    has_up = i + 2 < T
    has_dn = i >= 2
    has_far = i >= 4
    helps = jnp.logical_and(has_up, has_dn)
    scaling = HD ** (-0.5) * LOG2E

    w_copy = pltpu.make_async_copy(wqkv_hbm, wqkv, w_sem.at[0])
    w_copy.start()
    wo_copy = pltpu.make_async_copy(wout_hbm, wout, w_sem.at[1])
    wo_copy.start()
    barrier = pltpu.get_barrier_semaphore()
    for k in range(1, H):
        pl.semaphore_signal(barrier, inc=1, device_id={"head": lax.rem(h + k, H)}, device_id_type=MESH)
    pl.semaphore_signal(barrier, inc=1, device_id={"tok": mate}, device_id_type=MESH)

    @pl.when(has_up)
    def _():
        pl.semaphore_signal(barrier, inc=1, device_id={"tok": i + 2}, device_id_type=MESH)

    @pl.when(has_dn)
    def _():
        pl.semaphore_signal(barrier, inc=1, device_id={"tok": i - 2}, device_id_type=MESH)

    def to_own(lower, upper):
        return jnp.where(odd == 1, upper, lower), jnp.where(odd == 1, lower, upper)

    own_heads = pl.ds(odd * NL, NL)
    mate_heads = pl.ds((1 - odd) * NL, NL)
    pb[i] = pt[own_heads]
    def pre_up(b):
        return remote(pb.at[b], pb.at[b], pz_up.at[b], p_r.at[b], "tok", i + 2)

    def pre_dn(b):
        return remote(pb.at[b], pb.at[b], pz_dn.at[b], p_r.at[b], "tok", i - 2)

    def pre_mate():
        return remote(pt.at[mate_heads], pb.at[i], pp_s.at[0], p_r.at[i], "tok", mate)

    def pre_got(b):
        remote(pt.at[mate_heads], pb.at[b], pp_s.at[0], p_r.at[b], "tok", mate).wait_recv()

    def pre_spread(b):
        @pl.when(has_up)
        def _():
            pre_up(b).start()

        @pl.when(has_dn)
        def _():
            pre_dn(b).start()

    STEPS = NP - 1
    first_of = i - odd

    def pre_step(s, e):
        below = first_of - 2 * s + e
        above = first_of + 2 * s + e

        @pl.when(below >= 0)
        def _():
            pre_got(below)

            @pl.when(has_up)
            def _():
                pre_up(below).start()

        @pl.when(above < T)
        def _():
            pre_got(above)

            @pl.when(has_dn)
            def _():
                pre_dn(above).start()

    pending = [(s, e) for s in range(1, STEPS + 1) for e in (odd, 1 - odd)]

    def pre_next():
        if pending:
            pre_step(*pending.pop(0))

    ones_rows = jnp.ones((16, W), jnp.bfloat16)
    row_id = lax.broadcasted_iota(jnp.int32, (8, R), 0)
    base = hct[...]
    for j in range(STREAMS):
        s = streams[j]
        sf = s.astype(jnp.float32)
        sq = sf * sf
        hi = sq.astype(jnp.bfloat16)
        lo = (sq - hi.astype(jnp.float32)).astype(jnp.bfloat16)
        pr = lax.dot_general(base, s, NT, preferred_element_type=jnp.float32)
        sums = lax.dot_general(ones_rows, s, NT, preferred_element_type=jnp.float32)
        sqs = lax.dot_general(ones_rows, hi, NT, preferred_element_type=jnp.float32) + lax.dot_general(
            ones_rows, lo, NT, preferred_element_type=jnp.float32
        )
        stat[8 * j : 8 * j + 8, :] = jnp.where(row_id == 7, sqs[0:8], sums[0:8])
        stat[8 * j : 8 * j + COLS, :] = pr
    cs = lax.dot_general(base, jnp.ones((R, W), jnp.bfloat16), NT, preferred_element_type=jnp.float32)
    stat[32:40, :] = jnp.zeros((8, R), jnp.float32)
    stat[32 : 32 + COLS, :] = cs

    def stat_copy(k):
        return remote(stat, stat_in.at[k - 1], stat_ss.at[k - 1], stat_rs.at[k - 1], "head", lax.rem(h + k, H))

    pl.semaphore_wait(barrier, H + has_up.astype(jnp.int32) + has_dn.astype(jnp.int32))
    for k in range(1, H):
        stat_copy(k).start()
    pre_mate().start()
    pre_spread(i)

    sub = lax.broadcasted_iota(jnp.int32, (8, 2 * R), 0)
    pos = first_of * R + lax.broadcasted_iota(jnp.int32, (8, 2 * R), 1) + (1 - sub) * (2 * R)
    request = jnp.zeros((8, 2 * R), jnp.int32)
    begin = jnp.zeros((8, 2 * R), jnp.int32)
    group = jnp.full((8, 2 * R), reqgrp[0], jnp.int32)
    finish = jnp.int32(0)
    for q in range(NR):
        finish = finish + lengths[q]
        past = finish <= pos
        request = request + past.astype(jnp.int32)
        begin = jnp.where(past, finish, begin)
        group = jnp.where(past, reqgrp[min(q + 1, NR - 1)], group)
    keyreq[...] = request.astype(jnp.float32)
    inf[...] = jnp.zeros_like(inf)
    for row, values in enumerate((request, group, PRE + pos - begin)):
        inf[8 * row : 8 * row + 8, :] = jnp.where(sub <= 1, values, 0).astype(jnp.float32)
    inft[...] = jnp.transpose(inf[...])
    for b in range(T):
        pown[:, b * BR : (b + 1) * BR] = jnp.full((8, BR), prefgrp[b], jnp.int32).astype(jnp.float32)
    first_half = lax.broadcasted_iota(jnp.int32, (BR, HD), 1) < HD // 2
    for r in range(NB):
        rows = slice(r * BR, (r + 1) * BR)
        at = pl.ds(pl.multiple_of(odd * R + r * BR, BR), BR)
        angle = inft[at, 17:18] * freq[0:1, :]
        cosb[rows, :] = jnp.cos(angle)
        sine = jnp.sin(angle)
        sinb[rows, :] = jnp.where(first_half, -sine, sine)

    pre_got(mate)
    pre_spread(mate)
    for k in range(1, H):
        stat_copy(k).wait_recv()
    total = stat[...]
    for k in range(1, H):
        total = total + stat_in[k - 1]
    ctr[...] = jnp.zeros_like(ctr)
    col_sum = total[32:40]
    for j in range(STREAMS):
        blk = total[8 * j : 8 * j + 8]
        average = blk[6:7] / D
        spread = blk[7:8] / D - average * average
        inv = lax.rsqrt(spread + EPSILON)
        static = jnp.zeros((8, R), jnp.float32)
        for c in range(COLS):
            static = jnp.where(row_id == c, hstat[j, c], static)
        ctr[8 * j : 8 * j + 8, :] = jnp.tanh((blk - average * col_sum) * inv) + static
    coef[...] = jnp.transpose(ctr[...])

    def mix_y(r, k):
        to = lax.rem(yy + k, Y) * 2 + core
        return remote(mix.at[r, h], mix.at[r, h], mix_ys.at[r, k - 1], mix_yr.at[r, k - 1], "head", to)

    def mix_core(r, k):
        piece = lax.rem(yy + Y - k, Y) * 2 + core
        return remote(mix.at[r, piece], mix.at[r, piece], mix_cs.at[r, k], mix_cr.at[r, k], "head", other)

    for r in range(NB):
        rows = slice(r * BR, (r + 1) * BR)
        total_mix = None
        for j in range(STREAMS):
            term = coef[rows, 8 * j : 8 * j + 1] * streams[j, rows, :].astype(jnp.float32)
            total_mix = term if total_mix is None else total_mix + term
        mix[r, h] = total_mix.astype(jnp.bfloat16)
        for k in range(1, Y):
            mix_y(r, k).start()
        mix_core(r, 0).start()

    def own_share(r):
        rows = slice(r * BR, (r + 1) * BR)
        for q in range(STREAMS):
            share = None
            for j in range(STREAMS):
                term = coef[rows, 8 * j + 1 + q : 8 * j + 2 + q] * streams[j, rows, :].astype(jnp.float32)
                share = term if share is None else share + term
            upd[q, rows, :] = share

    pre_next()
    own_share(0)
    pre_next()

    mine = odd * NB
    theirs = (1 - odd) * NB

    def kv_mate(r):
        return remote(snd_kv.at[r], kvb.at[0, mine + r], ms_kv.at[r], k_r.at[0, mine + r], "tok", mate)

    def q_mate(r):
        return remote(snd_q.at[r], qb.at[mine + r], ms_q.at[r], q_r.at[mine + r], "tok", mate)

    def kv_got(level, c):
        remote(snd_kv.at[0], kvb.at[level, c], ms_kv.at[0], k_r.at[level, c], "tok", mate).wait_recv()

    def q_got(c):
        remote(snd_q.at[0], qb.at[c], ms_q.at[0], q_r.at[c], "tok", mate).wait_recv()

    def kv_up(level, c):
        return remote(kvb.at[level, c], kvb.at[level + 1, c], kz_s.at[level, c], k_r.at[level + 1, c], "tok", i + 2)

    def q_down(c):
        return remote(qb.at[c], qd.at[c], qd_s.at[c], qd_r.at[c], "tok", i - 2)

    def forward_kv(r):
        kv_got(0, theirs + r)

        @pl.when(has_up)
        def _():
            kv_up(0, theirs + r).start()

    def forward_q(r):
        q_got(theirs + r)

        @pl.when(has_far)
        def _():
            q_down(theirs + r).start()

    def weigh(query, key, value, allowed, floor):
        scores = lax.dot_general(query, key, NT, preferred_element_type=jnp.float32) * scaling
        scores = jnp.where(allowed, scores, MASKED)
        top = jnp.max(scores, 1, keepdims=True)
        if floor is not None:
            top = jnp.maximum(floor, top)
        weights = jnp.exp2(scores - top)
        count = jnp.sum(weights, 1, keepdims=True)
        return top, count, jnp.dot(weights.astype(jnp.bfloat16), value, preferred_element_type=jnp.float32)

    def attend(c, blocks, pieces, allowed, first):
        rows, at = blocks * BR, pl.ds(c, blocks)
        for n in range(NL):
            key, value = pieces(n)
            old = None if first else mb[n, at].reshape(rows, HD)[:, 0:1]
            query = qb[at, :, n * HD : (n + 1) * HD].reshape(rows, HD)
            top, count, numer = weigh(query, key, value, allowed, old)
            if not first:
                scale = jnp.exp2(old - top)
                count = count + lb[n, at].reshape(rows, HD)[:, 0:1] * scale
                numer = numer + acc[n, at].reshape(rows, HD) * scale
            mb[n, at] = jnp.broadcast_to(top, (rows, HD)).reshape(blocks, BR, HD)
            lb[n, at] = jnp.broadcast_to(count, (rows, HD)).reshape(blocks, BR, HD)
            acc[n, at] = numer.reshape(blocks, BR, HD)

    def row_info(c, blocks, column):
        return inft[pl.ds(pl.multiple_of(c * BR, BR), blocks * BR), column : column + 1]

    def absorb_prefix(c):
        for g in range((T + PG - 1) // PG):
            lo, hi = g * PG, min(T, (g + 1) * PG)

            def pieces(n):
                kv = pb[lo:hi, n].reshape((hi - lo) * BR, 2 * HD)
                return kv[:, 0:HD], kv[:, HD : 2 * HD]

            attend(c, NB, pieces, row_info(c, NB, 9) == pown[0:1, lo * BR : hi * BR], False)

    def kv_pieces(level, lo, blocks):
        def pieces(n):
            size, at = blocks * BR, pl.ds(lo, blocks)
            key = kvb[level, at, :, n * HD : (n + 1) * HD].reshape(size, HD)
            return key, kvb[level, at, :, W2 + n * HD : W2 + (n + 1) * HD].reshape(size, HD)

        return pieces

    def key_info(level, lo, blocks):
        return keyreq[level + 1 : level + 2, pl.ds(pl.multiple_of(lo * BR, BR), blocks * BR)]

    def absorb_own(first_block, r):
        size = (r + 1) * BR
        causal = lax.broadcasted_iota(jnp.int32, (BR, size), 1) <= lax.broadcasted_iota(jnp.int32, (BR, size), 0) + r * BR
        allowed = jnp.logical_and(row_info(first_block + r, 1, 1) == key_info(0, first_block, r + 1), causal)
        attend(first_block + r, 1, kv_pieces(0, first_block, r + 1), allowed, True)

    def absorb_cross():
        attend(NB, NB, kv_pieces(0, 0, NB), row_info(NB, NB, 1) == key_info(0, 0, NB), False)

    def absorb_below(c):
        attend(c, 1, kv_pieces(1, 0, C), row_info(c, 1, 1) == key_info(1, 0, C), False)

    lane = lax.broadcasted_iota(jnp.int32, (BR, HD), 1)

    def part_copies(c):
        return (
            remote(part_o.at[c], got_o.at[c], po_s.at[c], po_r.at[c], "tok", i + 2),
            remote(part_s.at[c], got_s.at[c], ps_s.at[c], ps_r.at[c], "tok", i + 2),
        )

    def help_up(c):
        pieces = kv_pieces(1, c, C - c)
        allowed = row_info(c, 1, 0) == key_info(1, c, C - c)
        remote(qb.at[c], qd.at[c], qd_s.at[c], qd_r.at[c], "tok", i + 2).wait_recv()
        sums = jnp.zeros((BR, HD), jnp.float32)
        for n in range(NL):
            key, value = pieces(n)
            top, count, numer = weigh(qd[c, :, n * HD : (n + 1) * HD], key, value, allowed, None)
            part_o[c, :, n * HD : (n + 1) * HD] = (numer / count).astype(jnp.bfloat16)
            sums = jnp.where(lane == n, top, jnp.where(lane == NL + n, count, sums))
        part_s[c] = jnp.transpose(sums)[0:8]
        for copy in part_copies(c):
            copy.start()

    def merge_part(c):
        for copy in part_copies(c):
            copy.wait_recv()
        sums = jnp.transpose(jnp.concatenate([got_s[c], jnp.zeros((HD - 8, BR), jnp.float32)], 0))
        for n in range(NL):
            far_top, far_count = sums[:, n : n + 1], sums[:, NL + n : NL + n + 1]
            old = mb[n, c][:, 0:1]
            top = jnp.maximum(old, far_top)
            scale = jnp.exp2(old - top)
            far = far_count * jnp.exp2(far_top - top)
            lb[n, c] = lb[n, c] * scale + far
            acc[n, c] = acc[n, c] * scale + got_o[c, :, n * HD : (n + 1) * HD].astype(jnp.float32) * far

    for r in range(NB):
        rows = slice(r * BR, (r + 1) * BR)
        for k in range(1, Y):
            mix_y(r, k).wait_recv()
            mix_core(r, k).start()
        for k in range(Y):
            mix_core(r, k).wait_recv()
        pre_next()
        if r == 0:
            w_copy.wait()
        summed = None
        for p in range(H):
            piece = jnp.sum(mix[r, p].astype(jnp.float32), -1, keepdims=True)
            summed = piece if summed is None else summed + piece
        center = summed / D
        squares = None
        for p in range(H):
            dev = mix[r, p].astype(jnp.float32) - center
            piece = jnp.sum(dev * dev, -1, keepdims=True)
            squares = piece if squares is None else squares + piece
        inv = lax.rsqrt(squares / D + EPSILON)
        for p in range(H):
            nrm[:, p * W : (p + 1) * W] = ((mix[r, p].astype(jnp.float32) - center) * inv).astype(jnp.bfloat16)
        c = cosb[rows, :]
        sn = sinb[rows, :]

        def rotated(values):
            parts = []
            for n in range(2 * NL):
                one = values[:, n * HD : (n + 1) * HD]
                parts.append(one * c + pltpu.roll(one, HD // 2, 1) * sn)
            return jnp.concatenate(parts, 1)

        kk = rotated(jnp.dot(nrm[...], wqkv[1], preferred_element_type=jnp.float32))
        vv = jnp.dot(nrm[...], wqkv[2], preferred_element_type=jnp.float32)
        k_loc, k_oth = to_own(kk[:, 0:W2], kk[:, W2:W])
        v_loc, v_oth = to_own(vv[:, 0:W2], vv[:, W2:W])
        snd_kv[r, :, 0:W2] = k_oth.astype(jnp.bfloat16)
        snd_kv[r, :, W2:W] = v_oth.astype(jnp.bfloat16)
        kv_mate(r).start()
        kvb[0, mine + r, :, 0:W2] = k_loc.astype(jnp.bfloat16)
        kvb[0, mine + r, :, W2:W] = v_loc.astype(jnp.bfloat16)

        @pl.when(has_up)
        def _():
            kv_up(0, mine + r).start()

        k_out[rows, :] = kk.astype(jnp.bfloat16)
        v_out[rows, :] = vv.astype(jnp.bfloat16)
        qq = rotated(jnp.dot(nrm[...], wqkv[0], preferred_element_type=jnp.float32))
        q_loc, q_oth = to_own(qq[:, 0:W2], qq[:, W2:W])
        snd_q[r] = q_oth.astype(jnp.bfloat16)
        q_mate(r).start()
        qb[mine + r] = q_loc.astype(jnp.bfloat16)

        @pl.when(has_far)
        def _():
            q_down(mine + r).start()

        absorb_own(mine, r)
        if r > 0:
            forward_kv(r - 1)
        if r > 1:
            forward_q(r - 2)
        pre_next()
    while pending:
        pre_next()

    absorb_prefix(mine)
    forward_kv(NB - 1)
    for r in range(max(0, NB - 2), NB):
        forward_q(r)
    for r in range(NB):
        absorb_own(theirs, r)
    absorb_prefix(theirs)
    absorb_cross()

    order = [c for r in reversed(range(NB)) for c in (NB + r, r)]

    for r in range(1, NB):
        own_share(r)

    @pl.when(has_dn)
    def _():
        for c in range(C):
            kv_got(1, c)

    @pl.when(helps)
    def _():
        for c in order:
            help_up(c)

    wo_copy.wait()

    def o_mate(r):
        return remote(ob.at[theirs + r], om.at[r], o_s.at[r], o_r.at[r], "tok", mate)

    def out_core(r):
        return remote(pair_out.at[r], pair_in.at[r], ro_cs.at[r], ro_cr.at[r], "head", other)

    def out_y(r, k):
        to = lax.rem(yy + k, Y)
        return remote(y_out.at[r, k - 1], y_in.at[r, k - 1], ro_ys.at[r, k - 1], ro_yr.at[r, k - 1], "head", to * 2 + core)

    own_rows = pl.ds(pl.multiple_of(odd * W2, HD), W2)
    mate_rows = pl.ds(pl.multiple_of((1 - odd) * W2, HD), W2)

    def finish_heads(c):
        @pl.when(has_dn)
        def _():
            absorb_below(c)

        @pl.when(has_far)
        def _():
            merge_part(c)

        for n in range(NL):
            ob[c, :, n * HD : (n + 1) * HD] = (acc[n, c] / lb[n, c]).astype(jnp.bfloat16)

        @pl.when(odd != c // NB)
        def _():
            o_mate(c % NB).start()

    def project(c):
        r = c % NB

        @pl.when(odd == c // NB)
        def _():
            o_mate(r).wait_recv()
            partial_rows = jnp.dot(ob[c], wout[own_rows, :], preferred_element_type=jnp.float32) + jnp.dot(
                om[r], wout[mate_rows, :], preferred_element_type=jnp.float32
            )
            for p in range(H):
                part[p, r] = partial_rows[:, p * W : (p + 1) * W]
            for q in range(Y):
                pair_out[r, q] = part[2 * q + 1 - core, r].astype(jnp.bfloat16)
            out_core(r).start()

    def pair_sum(c):
        r = c % NB

        @pl.when(odd == c // NB)
        def _():
            out_core(r).wait_recv()
            for k in range(1, Y):
                q = lax.rem(yy + k, Y)
                y_out[r, k - 1] = (part[2 * q + core, r] + pair_in[r, q].astype(jnp.float32)).astype(jnp.bfloat16)
                out_y(r, k).start()

    def update(r):
        rows = slice(r * BR, (r + 1) * BR)
        branch = part[h, r] + pair_in[r, yy].astype(jnp.float32)
        for k in range(1, Y):
            out_y(r, k).wait_recv()
            branch = branch + y_in[r, k - 1].astype(jnp.float32)
        for q in range(STREAMS):
            out[q, rows, :] = (upd[q, rows, :] + coef[rows, 8 * q + 5 : 8 * q + 6] * branch).astype(jnp.bfloat16)

    for at in range(C + 2):
        if at < C:
            finish_heads(order[at])
        if 1 <= at <= C:
            project(order[at - 1])
        if at >= 2:
            pair_sum(order[at - 2])
    for r in reversed(range(NB)):
        update(r)

    for k in range(1, H):
        stat_copy(k).wait_send()
    for r in range(NB):
        for k in range(1, Y):
            mix_y(r, k).wait_send()
        for k in range(Y):
            mix_core(r, k).wait_send()
        kv_mate(r).wait_send()
        q_mate(r).wait_send()
        o_mate(r).wait_send()
        out_core(r).wait_send()
        for k in range(1, Y):
            out_y(r, k).wait_send()

    @pl.when(has_up)
    def _():
        for c in range(C):
            kv_up(0, c).wait_send()

    @pl.when(helps)
    def _():
        for c in range(C):
            for copy in part_copies(c):
                copy.wait_send()

    @pl.when(has_far)
    def _():
        for c in range(C):
            q_down(c).wait_send()

    pre_mate().wait_send()

    def spread_done(b, up, down):
        @pl.when(jnp.logical_and(up, has_up))
        def _():
            pre_up(b).wait_send()

        @pl.when(jnp.logical_and(down, has_dn))
        def _():
            pre_dn(b).wait_send()

    for b in range(T):
        spread_done(b, b // 2 <= i // 2, b // 2 >= i // 2)


def shards(streams, hc_static, hc_proj, w_qkv, w_out, prefix_kv, lengths, req_group, prefix_group):
    R = streams.shape[0]
    W = streams.shape[2]
    D = w_qkv.shape[1]
    T = lax.axis_size("tok")
    H = lax.axis_size("head")
    NL = W // HD // 2
    W2 = W // 2
    NB = R // BR
    C = 2 * NB
    Y = H // 2
    assert R % BR == 0 and 4 * R >= MOST and T % 2 == 0 and prefix_kv.shape[0] == BR
    prefix_len = prefix_kv.shape[0] * T // GROUPS
    half = np.arange(HD // 2).astype(np.float32)
    freq = np.float32(ROPE_BASE) ** (-(half * np.float32(2.0) / np.float32(HD)))
    freq = jnp.asarray(np.tile(np.concatenate([freq, freq])[None, :], (8, 1)).astype(np.float32))
    streams_t = jnp.transpose(streams, (1, 0, 2))
    prefix_t = jnp.transpose(prefix_kv.reshape(BR, 2, 2 * NL, HD), (2, 0, 1, 3)).reshape(2 * NL, BR, 2 * HD)

    vm = pl.BlockSpec(memory_space=pltpu.VMEM)
    sm = pl.BlockSpec(memory_space=pltpu.SMEM)
    hbm = pl.BlockSpec(memory_space=pltpu.HBM)
    dma = pltpu.SemaphoreType.DMA
    bf, f32 = jnp.bfloat16, jnp.float32
    new_t, k_new, v_new = pl.pallas_call(
        functools.partial(kernel, T, H, R, W, D, lengths.shape[0], prefix_len),
        out_shape=(
            pltpu.VMEM((STREAMS, R, W), bf),
            pltpu.VMEM((R, W), bf),
            pltpu.VMEM((R, W), bf),
        ),
        in_specs=[vm, vm, sm, vm, sm, sm, sm, vm, hbm, hbm],
        out_specs=(vm, vm, vm),
        scratch_shapes=[
            pltpu.VMEM((3, D, W), bf),
            pltpu.VMEM((W, D), bf),
            pltpu.VMEM((40, R), f32),
            pltpu.VMEM((H - 1, 40, R), f32),
            pltpu.VMEM((128, R), f32),
            pltpu.VMEM((R, 128), f32),
            pltpu.VMEM((128, 2 * R), f32),
            pltpu.VMEM((2 * R, 128), f32),
            pltpu.VMEM((8, 2 * R), f32),
            pltpu.VMEM((8, T * BR), f32),
            pltpu.VMEM((R, HD), f32),
            pltpu.VMEM((R, HD), f32),
            pltpu.VMEM((NB, H, BR, W), bf),
            pltpu.VMEM((BR, D), bf),
            pltpu.VMEM((C, BR, W2), bf),
            pltpu.VMEM((2, C, BR, W), bf),
            pltpu.VMEM((NB, BR, W), bf),
            pltpu.VMEM((NB, BR, W2), bf),
            pltpu.VMEM((C, BR, W2), bf),
            pltpu.VMEM((T, NL, BR, 2 * HD), bf),
            pltpu.VMEM((NL, C, BR, HD), f32),
            pltpu.VMEM((NL, C, BR, HD), f32),
            pltpu.VMEM((NL, C, BR, HD), f32),
            pltpu.VMEM((C, BR, W2), bf),
            pltpu.VMEM((C, 8, BR), f32),
            pltpu.VMEM((C, BR, W2), bf),
            pltpu.VMEM((C, 8, BR), f32),
            pltpu.VMEM((C, BR, W2), bf),
            pltpu.VMEM((NB, BR, W2), bf),
            pltpu.VMEM((STREAMS, R, W), f32),
            pltpu.VMEM((H, NB, BR, W), f32),
            pltpu.VMEM((NB, Y, BR, W), bf),
            pltpu.VMEM((NB, Y, BR, W), bf),
            pltpu.VMEM((NB, Y - 1, BR, W), bf),
            pltpu.VMEM((NB, Y - 1, BR, W), bf),
            dma((2,)),
            dma((H - 1,)),
            dma((H - 1,)),
            dma((NB, Y - 1)),
            dma((NB, Y - 1)),
            dma((NB, Y)),
            dma((NB, Y)),
            dma((T,)),
            dma((T,)),
            dma((1,)),
            dma((T,)),
            dma((NB,)),
            dma((NB,)),
            dma((C,)),
            dma((1, C)),
            dma((2, C)),
            dma((C,)),
            dma((C,)),
            dma((C,)),
            dma((C,)),
            dma((C,)),
            dma((C,)),
            dma((NB,)),
            dma((NB,)),
            dma((NB,)),
            dma((NB,)),
            dma((NB, Y - 1)),
            dma((NB, Y - 1)),
        ],
        compiler_params=pltpu.CompilerParams(
            collective_id=0, has_side_effects=True, vmem_limit_bytes=44 * 1024 * 1024
        ),
    )(
        streams_t, hc_proj.T, hc_static, freq, lengths, req_group, prefix_group,
        prefix_t, w_qkv, w_out,
    )
    return jnp.transpose(new_t, (1, 0, 2)), jnp.stack([k_new, v_new], 1)


def solution(mesh):
    in_specs = (
        P("tok", None, "head"),
        P(),
        P("head", None),
        P(None, None, "head"),
        P("head", None),
        P("tok", None, "head"),
        P(),
        P(),
        P(),
    )
    out_specs = (P("tok", None, "head"), P("tok", None, "head"))
    return jax.shard_map(shards, mesh=mesh, in_specs=in_specs, out_specs=out_specs, check_vma=False)
```

```python
import functools

import jax
import jax.numpy as jnp
import numpy as np
from jax import lax
from jax.experimental import pallas as pl
from jax.experimental.pallas import tpu as pltpu
from jax.sharding import PartitionSpec as P

HD = 128
STREAMS = 4
GROUPS = 4
COLS = STREAMS + 2
MOST = 1536
BR = 128
PG = 8

EPSILON = 1e-05
MASKED = -1e30
ROPE_BASE = 10000.0
LOG2E = 1.4426950408889634
MESH = pl.DeviceIdType.MESH
NT = (((1,), (1,)), ((), ()))


def remote(src, dst, send_sem, recv_sem, axis, target):
    return pltpu.make_async_remote_copy(
        src_ref=src,
        dst_ref=dst,
        send_sem=send_sem,
        recv_sem=recv_sem,
        device_id={axis: target},
        device_id_type=MESH,
    )


def kernel(
    T, H, R, W, D, NR, PRE,
    streams, hct, hstat, freq, lengths, reqgrp, prefgrp, pt, wqkv_hbm, wout_hbm,
    out, kv_out,
    wqkv, wout, stat, stat_in, ctr, coef, inf, inft, keyreq, pown, cosb, sinb, mix, nrm, qb, kvb, snd_kv, snd_q, qd, pb,
    mb, lb, acc, part_o, part_s, got_o, got_s, ob, om, upd, part, pair_out, pair_in, y_out, y_in,
    w_sem, stat_ss, stat_rs, mix_ys, mix_yr, mix_cs, mix_cr, pz_up, pz_dn, pp_s, p_r, ms_kv, ms_q, q_r, kz_s, k_r, qd_s, qd_r, po_s, po_r, ps_s, ps_r,
    o_s, o_r, ro_cs, ro_cr, ro_ys, ro_yr,
):
    NB = R // BR
    C = 2 * NB
    NL = W // HD // 2
    W2 = W // 2
    Y = H // 2
    NP = T // 2
    i = lax.axis_index("tok")
    h = lax.axis_index("head")
    core = lax.rem(h, 2)
    yy = h // 2
    other = h + 1 - 2 * core
    odd = lax.rem(i, 2)
    mate = i + 1 - 2 * odd
    has_up = i + 2 < T
    has_dn = i >= 2
    has_far = i >= 4
    helps = jnp.logical_and(has_up, has_dn)
    scaling = HD ** (-0.5) * LOG2E

    w_copy = pltpu.make_async_copy(wqkv_hbm, wqkv, w_sem.at[0])
    w_copy.start()
    wo_copy = pltpu.make_async_copy(wout_hbm, wout, w_sem.at[1])
    wo_copy.start()
    barrier = pltpu.get_barrier_semaphore()
    for k in range(1, H):
        pl.semaphore_signal(barrier, inc=1, device_id={"head": lax.rem(h + k, H)}, device_id_type=MESH)
    pl.semaphore_signal(barrier, inc=1, device_id={"tok": mate}, device_id_type=MESH)

    @pl.when(has_up)
    def _():
        pl.semaphore_signal(barrier, inc=1, device_id={"tok": i + 2}, device_id_type=MESH)

    @pl.when(has_dn)
    def _():
        pl.semaphore_signal(barrier, inc=1, device_id={"tok": i - 2}, device_id_type=MESH)

    def to_own(lower, upper):
        return jnp.where(odd == 1, upper, lower), jnp.where(odd == 1, lower, upper)

    own_heads = pl.ds(odd * NL, NL)
    mate_heads = pl.ds((1 - odd) * NL, NL)
    pb[i] = pt[own_heads]
    def pre_up(b):
        return remote(pb.at[b], pb.at[b], pz_up.at[b], p_r.at[b], "tok", i + 2)

    def pre_dn(b):
        return remote(pb.at[b], pb.at[b], pz_dn.at[b], p_r.at[b], "tok", i - 2)

    def pre_mate():
        return remote(pt.at[mate_heads], pb.at[i], pp_s.at[0], p_r.at[i], "tok", mate)

    def pre_got(b):
        remote(pt.at[mate_heads], pb.at[b], pp_s.at[0], p_r.at[b], "tok", mate).wait_recv()

    def pre_spread(b):
        @pl.when(has_up)
        def _():
            pre_up(b).start()

        @pl.when(has_dn)
        def _():
            pre_dn(b).start()

    STEPS = NP - 1
    first_of = i - odd

    def pre_step(s, e):
        below = first_of - 2 * s + e
        above = first_of + 2 * s + e

        @pl.when(below >= 0)
        def _():
            pre_got(below)

            @pl.when(has_up)
            def _():
                pre_up(below).start()

        @pl.when(above < T)
        def _():
            pre_got(above)

            @pl.when(has_dn)
            def _():
                pre_dn(above).start()

    pending = [(s, e) for s in range(1, STEPS + 1) for e in (odd, 1 - odd)]

    def pre_next():
        if pending:
            pre_step(*pending.pop(0))

    ones_rows = jnp.ones((16, W), jnp.bfloat16)
    row_id = lax.broadcasted_iota(jnp.int32, (8, R), 0)
    base = hct[...]
    for j in range(STREAMS):
        s = streams[j]
        sf = s.astype(jnp.float32)
        sq = sf * sf
        hi = sq.astype(jnp.bfloat16)
        lo = (sq - hi.astype(jnp.float32)).astype(jnp.bfloat16)
        pr = lax.dot_general(base, s, NT, preferred_element_type=jnp.float32)
        sums = lax.dot_general(ones_rows, s, NT, preferred_element_type=jnp.float32)
        sqs = lax.dot_general(ones_rows, hi, NT, preferred_element_type=jnp.float32) + lax.dot_general(
            ones_rows, lo, NT, preferred_element_type=jnp.float32
        )
        stat[8 * j : 8 * j + 8, :] = jnp.where(row_id == 7, sqs[0:8], sums[0:8])
        stat[8 * j : 8 * j + COLS, :] = pr
    cs = lax.dot_general(base, jnp.ones((R, W), jnp.bfloat16), NT, preferred_element_type=jnp.float32)
    stat[32:40, :] = jnp.zeros((8, R), jnp.float32)
    stat[32 : 32 + COLS, :] = cs

    def stat_copy(k):
        return remote(stat, stat_in.at[k - 1], stat_ss.at[k - 1], stat_rs.at[k - 1], "head", lax.rem(h + k, H))

    pl.semaphore_wait(barrier, H + has_up.astype(jnp.int32) + has_dn.astype(jnp.int32))
    for k in range(1, H):
        stat_copy(k).start()
    pre_mate().start()
    pre_spread(i)

    sub = lax.broadcasted_iota(jnp.int32, (8, 2 * R), 0)
    pos = first_of * R + lax.broadcasted_iota(jnp.int32, (8, 2 * R), 1) + (1 - sub) * (2 * R)
    request = jnp.zeros((8, 2 * R), jnp.int32)
    begin = jnp.zeros((8, 2 * R), jnp.int32)
    group = jnp.full((8, 2 * R), reqgrp[0], jnp.int32)
    finish = jnp.int32(0)
    for q in range(NR):
        finish = finish + lengths[q]
        past = finish <= pos
        request = request + past.astype(jnp.int32)
        begin = jnp.where(past, finish, begin)
        group = jnp.where(past, reqgrp[min(q + 1, NR - 1)], group)
    keyreq[...] = request.astype(jnp.float32)
    inf[...] = jnp.zeros_like(inf)
    for row, values in enumerate((request, group, PRE + pos - begin)):
        inf[8 * row : 8 * row + 8, :] = jnp.where(sub <= 1, values, 0).astype(jnp.float32)
    inft[...] = jnp.transpose(inf[...])
    for b in range(T):
        pown[:, b * BR : (b + 1) * BR] = jnp.full((8, BR), prefgrp[b], jnp.int32).astype(jnp.float32)
    first_half = lax.broadcasted_iota(jnp.int32, (BR, HD), 1) < HD // 2
    for r in range(NB):
        rows = slice(r * BR, (r + 1) * BR)
        at = pl.ds(pl.multiple_of(odd * R + r * BR, BR), BR)
        angle = inft[at, 17:18] * freq[0:1, :]
        cosb[rows, :] = jnp.cos(angle)
        sine = jnp.sin(angle)
        sinb[rows, :] = jnp.where(first_half, -sine, sine)

    pre_got(mate)
    pre_spread(mate)
    for k in range(1, H):
        stat_copy(k).wait_recv()
    total = stat[...]
    for k in range(1, H):
        total = total + stat_in[k - 1]
    ctr[...] = jnp.zeros_like(ctr)
    col_sum = total[32:40]
    for j in range(STREAMS):
        blk = total[8 * j : 8 * j + 8]
        average = blk[6:7] / D
        spread = blk[7:8] / D - average * average
        inv = lax.rsqrt(spread + EPSILON)
        static = jnp.zeros((8, R), jnp.float32)
        for c in range(COLS):
            static = jnp.where(row_id == c, hstat[j, c], static)
        ctr[8 * j : 8 * j + 8, :] = jnp.tanh((blk - average * col_sum) * inv) + static
    coef[...] = jnp.transpose(ctr[...])

    def mix_y(r, k):
        to = lax.rem(yy + k, Y) * 2 + core
        return remote(mix.at[r, h], mix.at[r, h], mix_ys.at[r, k - 1], mix_yr.at[r, k - 1], "head", to)

    def mix_core(r, k):
        piece = lax.rem(yy + Y - k, Y) * 2 + core
        return remote(mix.at[r, piece], mix.at[r, piece], mix_cs.at[r, k], mix_cr.at[r, k], "head", other)

    for r in range(NB):
        rows = slice(r * BR, (r + 1) * BR)
        total_mix = None
        for j in range(STREAMS):
            term = coef[rows, 8 * j : 8 * j + 1] * streams[j, rows, :].astype(jnp.float32)
            total_mix = term if total_mix is None else total_mix + term
        mix[r, h] = total_mix.astype(jnp.bfloat16)
        for k in range(1, Y):
            mix_y(r, k).start()
        mix_core(r, 0).start()

    def own_share(r):
        rows = slice(r * BR, (r + 1) * BR)
        for q in range(STREAMS):
            share = None
            for j in range(STREAMS):
                term = coef[rows, 8 * j + 1 + q : 8 * j + 2 + q] * streams[j, rows, :].astype(jnp.float32)
                share = term if share is None else share + term
            upd[q, rows, :] = share

    pre_next()
    own_share(0)
    pre_next()

    mine = odd * NB
    theirs = (1 - odd) * NB

    def kv_mate(r):
        return remote(snd_kv.at[r], kvb.at[0, mine + r], ms_kv.at[r], k_r.at[0, mine + r], "tok", mate)

    def q_mate(r):
        return remote(snd_q.at[r], qb.at[mine + r], ms_q.at[r], q_r.at[mine + r], "tok", mate)

    def kv_got(level, c):
        remote(snd_kv.at[0], kvb.at[level, c], ms_kv.at[0], k_r.at[level, c], "tok", mate).wait_recv()

    def q_got(c):
        remote(snd_q.at[0], qb.at[c], ms_q.at[0], q_r.at[c], "tok", mate).wait_recv()

    def kv_up(level, c):
        return remote(kvb.at[level, c], kvb.at[level + 1, c], kz_s.at[level, c], k_r.at[level + 1, c], "tok", i + 2)

    def q_down(c):
        return remote(qb.at[c], qd.at[c], qd_s.at[c], qd_r.at[c], "tok", i - 2)

    def forward_kv(r):
        kv_got(0, theirs + r)

        @pl.when(has_up)
        def _():
            kv_up(0, theirs + r).start()

    def forward_q(r):
        q_got(theirs + r)

        @pl.when(has_far)
        def _():
            q_down(theirs + r).start()

    def weigh(query, key, value, allowed, floor):
        scores = lax.dot_general(query, key, NT, preferred_element_type=jnp.float32) * scaling
        scores = jnp.where(allowed, scores, MASKED)
        top = jnp.max(scores, 1, keepdims=True)
        if floor is not None:
            top = jnp.maximum(floor, top)
        weights = jnp.exp2(scores - top)
        count = jnp.sum(weights, 1, keepdims=True)
        return top, count, jnp.dot(weights.astype(jnp.bfloat16), value, preferred_element_type=jnp.float32)

    def attend(c, blocks, pieces, allowed, first):
        rows, at = blocks * BR, pl.ds(c, blocks)
        for n in range(NL):
            key, value = pieces(n)
            old = None if first else mb[n, at].reshape(rows, HD)[:, 0:1]
            query = qb[at, :, n * HD : (n + 1) * HD].reshape(rows, HD)
            top, count, numer = weigh(query, key, value, allowed, old)
            if not first:
                scale = jnp.exp2(old - top)
                count = count + lb[n, at].reshape(rows, HD)[:, 0:1] * scale
                numer = numer + acc[n, at].reshape(rows, HD) * scale
            mb[n, at] = jnp.broadcast_to(top, (rows, HD)).reshape(blocks, BR, HD)
            lb[n, at] = jnp.broadcast_to(count, (rows, HD)).reshape(blocks, BR, HD)
            acc[n, at] = numer.reshape(blocks, BR, HD)

    def row_info(c, blocks, column):
        return inft[pl.ds(pl.multiple_of(c * BR, BR), blocks * BR), column : column + 1]

    def absorb_prefix(c):
        for g in range((T + PG - 1) // PG):
            lo, hi = g * PG, min(T, (g + 1) * PG)

            def pieces(n):
                kv = pb[lo:hi, n].reshape((hi - lo) * BR, 2 * HD)
                return kv[:, 0:HD], kv[:, HD : 2 * HD]

            attend(c, NB, pieces, row_info(c, NB, 9) == pown[0:1, lo * BR : hi * BR], False)

    def kv_pieces(level, lo, blocks):
        def pieces(n):
            size, at = blocks * BR, pl.ds(lo, blocks)
            key = kvb[level, at, :, n * HD : (n + 1) * HD].reshape(size, HD)
            return key, kvb[level, at, :, W2 + n * HD : W2 + (n + 1) * HD].reshape(size, HD)

        return pieces

    def key_info(level, lo, blocks):
        return keyreq[level + 1 : level + 2, pl.ds(pl.multiple_of(lo * BR, BR), blocks * BR)]

    def absorb_own(first_block, r):
        size = (r + 1) * BR
        causal = lax.broadcasted_iota(jnp.int32, (BR, size), 1) <= lax.broadcasted_iota(jnp.int32, (BR, size), 0) + r * BR
        allowed = jnp.logical_and(row_info(first_block + r, 1, 1) == key_info(0, first_block, r + 1), causal)
        attend(first_block + r, 1, kv_pieces(0, first_block, r + 1), allowed, True)

    def absorb_cross():
        attend(NB, NB, kv_pieces(0, 0, NB), row_info(NB, NB, 1) == key_info(0, 0, NB), False)

    def absorb_below(c):
        attend(c, 1, kv_pieces(1, 0, C), row_info(c, 1, 1) == key_info(1, 0, C), False)

    lane = lax.broadcasted_iota(jnp.int32, (BR, HD), 1)

    def part_copies(c):
        return (
            remote(part_o.at[c], got_o.at[c], po_s.at[c], po_r.at[c], "tok", i + 2),
            remote(part_s.at[c], got_s.at[c], ps_s.at[c], ps_r.at[c], "tok", i + 2),
        )

    def help_up(c):
        pieces = kv_pieces(1, c, C - c)
        allowed = row_info(c, 1, 0) == key_info(1, c, C - c)
        remote(qb.at[c], qd.at[c], qd_s.at[c], qd_r.at[c], "tok", i + 2).wait_recv()
        sums = jnp.zeros((BR, HD), jnp.float32)
        for n in range(NL):
            key, value = pieces(n)
            top, count, numer = weigh(qd[c, :, n * HD : (n + 1) * HD], key, value, allowed, None)
            part_o[c, :, n * HD : (n + 1) * HD] = (numer / count).astype(jnp.bfloat16)
            sums = jnp.where(lane == n, top, jnp.where(lane == NL + n, count, sums))
        part_s[c] = jnp.transpose(sums)[0:8]
        for copy in part_copies(c):
            copy.start()

    def merge_part(c):
        for copy in part_copies(c):
            copy.wait_recv()
        sums = jnp.transpose(jnp.concatenate([got_s[c], jnp.zeros((HD - 8, BR), jnp.float32)], 0))
        for n in range(NL):
            far_top, far_count = sums[:, n : n + 1], sums[:, NL + n : NL + n + 1]
            old = mb[n, c][:, 0:1]
            top = jnp.maximum(old, far_top)
            scale = jnp.exp2(old - top)
            far = far_count * jnp.exp2(far_top - top)
            lb[n, c] = lb[n, c] * scale + far
            acc[n, c] = acc[n, c] * scale + got_o[c, :, n * HD : (n + 1) * HD].astype(jnp.float32) * far

    for r in range(NB):
        rows = slice(r * BR, (r + 1) * BR)
        for k in range(1, Y):
            mix_y(r, k).wait_recv()
            mix_core(r, k).start()
        for k in range(Y):
            mix_core(r, k).wait_recv()
        pre_next()
        if r == 0:
            w_copy.wait()
        summed = None
        for p in range(H):
            piece = jnp.sum(mix[r, p].astype(jnp.float32), -1, keepdims=True)
            summed = piece if summed is None else summed + piece
        center = summed / D
        squares = None
        for p in range(H):
            dev = mix[r, p].astype(jnp.float32) - center
            piece = jnp.sum(dev * dev, -1, keepdims=True)
            squares = piece if squares is None else squares + piece
        inv = lax.rsqrt(squares / D + EPSILON)
        for p in range(H):
            nrm[:, p * W : (p + 1) * W] = ((mix[r, p].astype(jnp.float32) - center) * inv).astype(jnp.bfloat16)
        c = cosb[rows, :]
        sn = sinb[rows, :]

        def rotated(values):
            parts = []
            for n in range(2 * NL):
                one = values[:, n * HD : (n + 1) * HD]
                parts.append(one * c + pltpu.roll(one, HD // 2, 1) * sn)
            return jnp.concatenate(parts, 1)

        kk = rotated(jnp.dot(nrm[...], wqkv[1], preferred_element_type=jnp.float32))
        vv = jnp.dot(nrm[...], wqkv[2], preferred_element_type=jnp.float32)
        k_loc, k_oth = to_own(kk[:, 0:W2], kk[:, W2:W])
        v_loc, v_oth = to_own(vv[:, 0:W2], vv[:, W2:W])
        snd_kv[r, :, 0:W2] = k_oth.astype(jnp.bfloat16)
        snd_kv[r, :, W2:W] = v_oth.astype(jnp.bfloat16)
        kv_mate(r).start()
        kvb[0, mine + r, :, 0:W2] = k_loc.astype(jnp.bfloat16)
        kvb[0, mine + r, :, W2:W] = v_loc.astype(jnp.bfloat16)

        @pl.when(has_up)
        def _():
            kv_up(0, mine + r).start()

        qq = rotated(jnp.dot(nrm[...], wqkv[0], preferred_element_type=jnp.float32))
        q_loc, q_oth = to_own(qq[:, 0:W2], qq[:, W2:W])
        snd_q[r] = q_oth.astype(jnp.bfloat16)
        q_mate(r).start()
        qb[mine + r] = q_loc.astype(jnp.bfloat16)

        @pl.when(has_far)
        def _():
            q_down(mine + r).start()

        kv_out[rows] = jnp.stack([kk, vv], 1).astype(jnp.bfloat16)
        absorb_own(mine, r)
        if r > 0:
            forward_kv(r - 1)
        if r > 1:
            forward_q(r - 2)
        pre_next()
    while pending:
        pre_next()

    absorb_prefix(mine)
    forward_kv(NB - 1)
    for r in range(max(0, NB - 2), NB):
        forward_q(r)
    for r in range(NB):
        absorb_own(theirs, r)
    absorb_prefix(theirs)
    absorb_cross()

    order = [c for r in reversed(range(NB)) for c in (NB + r, r)]

    for r in range(1, NB):
        own_share(r)

    @pl.when(has_dn)
    def _():
        for c in range(C):
            kv_got(1, c)

    @pl.when(helps)
    def _():
        for c in order:
            help_up(c)

    wo_copy.wait()

    def o_mate(r):
        return remote(ob.at[theirs + r], om.at[r], o_s.at[r], o_r.at[r], "tok", mate)

    def out_core(r):
        return remote(pair_out.at[r], pair_in.at[r], ro_cs.at[r], ro_cr.at[r], "head", other)

    def out_y(r, k):
        to = lax.rem(yy + k, Y)
        return remote(y_out.at[r, k - 1], y_in.at[r, k - 1], ro_ys.at[r, k - 1], ro_yr.at[r, k - 1], "head", to * 2 + core)

    own_rows = pl.ds(pl.multiple_of(odd * W2, HD), W2)
    mate_rows = pl.ds(pl.multiple_of((1 - odd) * W2, HD), W2)

    def finish_heads(c):
        @pl.when(has_dn)
        def _():
            absorb_below(c)

        @pl.when(has_far)
        def _():
            merge_part(c)

        for n in range(NL):
            ob[c, :, n * HD : (n + 1) * HD] = (acc[n, c] / lb[n, c]).astype(jnp.bfloat16)

        @pl.when(odd != c // NB)
        def _():
            o_mate(c % NB).start()

    def project(c):
        r = c % NB

        @pl.when(odd == c // NB)
        def _():
            o_mate(r).wait_recv()
            partial_rows = jnp.dot(ob[c], wout[own_rows, :], preferred_element_type=jnp.float32) + jnp.dot(
                om[r], wout[mate_rows, :], preferred_element_type=jnp.float32
            )
            for p in range(H):
                part[p, r] = partial_rows[:, p * W : (p + 1) * W]
            for q in range(Y):
                pair_out[r, q] = part[2 * q + 1 - core, r].astype(jnp.bfloat16)
            out_core(r).start()

    def pair_sum(c):
        r = c % NB

        @pl.when(odd == c // NB)
        def _():
            out_core(r).wait_recv()
            for k in range(1, Y):
                q = lax.rem(yy + k, Y)
                y_out[r, k - 1] = (part[2 * q + core, r] + pair_in[r, q].astype(jnp.float32)).astype(jnp.bfloat16)
                out_y(r, k).start()

    def update(r):
        rows = slice(r * BR, (r + 1) * BR)
        branch = part[h, r] + pair_in[r, yy].astype(jnp.float32)
        for k in range(1, Y):
            out_y(r, k).wait_recv()
            branch = branch + y_in[r, k - 1].astype(jnp.float32)
        for q in range(STREAMS):
            out[q, rows, :] = (upd[q, rows, :] + coef[rows, 8 * q + 5 : 8 * q + 6] * branch).astype(jnp.bfloat16)

    for at in range(C + 2):
        if at < C:
            finish_heads(order[at])
        if 1 <= at <= C:
            project(order[at - 1])
        if at >= 2:
            pair_sum(order[at - 2])
    for r in reversed(range(NB)):
        update(r)

    for k in range(1, H):
        stat_copy(k).wait_send()
    for r in range(NB):
        for k in range(1, Y):
            mix_y(r, k).wait_send()
        for k in range(Y):
            mix_core(r, k).wait_send()
        kv_mate(r).wait_send()
        q_mate(r).wait_send()
        o_mate(r).wait_send()
        out_core(r).wait_send()
        for k in range(1, Y):
            out_y(r, k).wait_send()

    @pl.when(has_up)
    def _():
        for c in range(C):
            kv_up(0, c).wait_send()

    @pl.when(helps)
    def _():
        for c in range(C):
            for copy in part_copies(c):
                copy.wait_send()

    @pl.when(has_far)
    def _():
        for c in range(C):
            q_down(c).wait_send()

    pre_mate().wait_send()

    def spread_done(b, up, down):
        @pl.when(jnp.logical_and(up, has_up))
        def _():
            pre_up(b).wait_send()

        @pl.when(jnp.logical_and(down, has_dn))
        def _():
            pre_dn(b).wait_send()

    for b in range(T):
        spread_done(b, b // 2 <= i // 2, b // 2 >= i // 2)


def shards(streams, hc_static, hc_proj, w_qkv, w_out, prefix_kv, lengths, req_group, prefix_group):
    R = streams.shape[0]
    W = streams.shape[2]
    D = w_qkv.shape[1]
    T = lax.axis_size("tok")
    H = lax.axis_size("head")
    NL = W // HD // 2
    W2 = W // 2
    NB = R // BR
    C = 2 * NB
    Y = H // 2
    assert R % BR == 0 and 4 * R >= MOST and T % 2 == 0 and prefix_kv.shape[0] == BR
    prefix_len = prefix_kv.shape[0] * T // GROUPS
    half = np.arange(HD // 2).astype(np.float32)
    freq = np.float32(ROPE_BASE) ** (-(half * np.float32(2.0) / np.float32(HD)))
    freq = jnp.asarray(np.tile(np.concatenate([freq, freq])[None, :], (8, 1)).astype(np.float32))
    streams_t = jnp.transpose(streams, (1, 0, 2))
    prefix_t = jnp.transpose(prefix_kv.reshape(BR, 2, 2 * NL, HD), (2, 0, 1, 3)).reshape(2 * NL, BR, 2 * HD)

    vm = pl.BlockSpec(memory_space=pltpu.VMEM)
    sm = pl.BlockSpec(memory_space=pltpu.SMEM)
    hbm = pl.BlockSpec(memory_space=pltpu.HBM)
    dma = pltpu.SemaphoreType.DMA
    bf, f32 = jnp.bfloat16, jnp.float32
    new_t, kv_new = pl.pallas_call(
        functools.partial(kernel, T, H, R, W, D, lengths.shape[0], prefix_len),
        out_shape=(
            pltpu.VMEM((STREAMS, R, W), bf),
            pltpu.VMEM((R, 2, W), bf),
        ),
        in_specs=[vm, vm, sm, vm, sm, sm, sm, vm, hbm, hbm],
        out_specs=(vm, vm),
        scratch_shapes=[
            pltpu.VMEM((3, D, W), bf),
            pltpu.VMEM((W, D), bf),
            pltpu.VMEM((40, R), f32),
            pltpu.VMEM((H - 1, 40, R), f32),
            pltpu.VMEM((128, R), f32),
            pltpu.VMEM((R, 128), f32),
            pltpu.VMEM((128, 2 * R), f32),
            pltpu.VMEM((2 * R, 128), f32),
            pltpu.VMEM((8, 2 * R), f32),
            pltpu.VMEM((8, T * BR), f32),
            pltpu.VMEM((R, HD), f32),
            pltpu.VMEM((R, HD), f32),
            pltpu.VMEM((NB, H, BR, W), bf),
            pltpu.VMEM((BR, D), bf),
            pltpu.VMEM((C, BR, W2), bf),
            pltpu.VMEM((2, C, BR, W), bf),
            pltpu.VMEM((NB, BR, W), bf),
            pltpu.VMEM((NB, BR, W2), bf),
            pltpu.VMEM((C, BR, W2), bf),
            pltpu.VMEM((T, NL, BR, 2 * HD), bf),
            pltpu.VMEM((NL, C, BR, HD), f32),
            pltpu.VMEM((NL, C, BR, HD), f32),
            pltpu.VMEM((NL, C, BR, HD), f32),
            pltpu.VMEM((C, BR, W2), bf),
            pltpu.VMEM((C, 8, BR), f32),
            pltpu.VMEM((C, BR, W2), bf),
            pltpu.VMEM((C, 8, BR), f32),
            pltpu.VMEM((C, BR, W2), bf),
            pltpu.VMEM((NB, BR, W2), bf),
            pltpu.VMEM((STREAMS, R, W), f32),
            pltpu.VMEM((H, NB, BR, W), f32),
            pltpu.VMEM((NB, Y, BR, W), bf),
            pltpu.VMEM((NB, Y, BR, W), bf),
            pltpu.VMEM((NB, Y - 1, BR, W), bf),
            pltpu.VMEM((NB, Y - 1, BR, W), bf),
            dma((2,)),
            dma((H - 1,)),
            dma((H - 1,)),
            dma((NB, Y - 1)),
            dma((NB, Y - 1)),
            dma((NB, Y)),
            dma((NB, Y)),
            dma((T,)),
            dma((T,)),
            dma((1,)),
            dma((T,)),
            dma((NB,)),
            dma((NB,)),
            dma((C,)),
            dma((1, C)),
            dma((2, C)),
            dma((C,)),
            dma((C,)),
            dma((C,)),
            dma((C,)),
            dma((C,)),
            dma((C,)),
            dma((NB,)),
            dma((NB,)),
            dma((NB,)),
            dma((NB,)),
            dma((NB, Y - 1)),
            dma((NB, Y - 1)),
        ],
        compiler_params=pltpu.CompilerParams(
            collective_id=0, has_side_effects=True, vmem_limit_bytes=44 * 1024 * 1024
        ),
    )(
        streams_t, hc_proj.T, hc_static, freq, lengths, req_group, prefix_group,
        prefix_t, w_qkv, w_out,
    )
    return jnp.transpose(new_t, (1, 0, 2)), kv_new


def solution(mesh):
    in_specs = (
        P("tok", None, "head"),
        P(),
        P("head", None),
        P(None, None, "head"),
        P("head", None),
        P("tok", None, "head"),
        P(),
        P(),
        P(),
    )
    out_specs = (P("tok", None, "head"), P("tok", None, "head"))
    return jax.shard_map(shards, mesh=mesh, in_specs=in_specs, out_specs=out_specs, check_vma=False)
```
